32 devices in a mesh: shard: 2 (over y), seq: 16 (over z, x, core).
Axes of the slice: x: 2, y: 2, z: 4, core: 2. Of those that a mesh axis runs over, the one named last changes fastest.
Arguments:
- queries: bfloat16 [16384, 1024], P(('shard', 'seq')), parts along dimension 0, may hold values from -112 to 112
- key_rows: bfloat16 [16384, 128], P(('shard', 'seq')), parts along dimension 0, may hold values from -4 to 4
- value_rows: bfloat16 [16384, 128], P(('shard', 'seq')), parts along dimension 0, may hold values from -6 to 6
- out_grads: bfloat16 [16384, 1024], P(('shard', 'seq')), parts along dimension 0, may hold values from -6 to 6
- segment_ids: int32 [16384], P('shard'), parts along dimension 0, may hold values from 0 to 1, never falling along the last dimension, each value on 1 to 7168 neighbouring positions
- random_blocks: int32 [128, 8, 3], P(('shard', 'seq')), parts along dimension 0, may hold values from 0 to 63, as said below
- global_blocks: int32 [4], P('shard'), parts along dimension 0, may hold values from 0 to 63
Outputs:
- attended: bfloat16 [16384, 1024], P(('shard', 'seq')), parts along dimension 0
- d_queries: bfloat16 [16384, 1024], P(('shard', 'seq')), parts along dimension 0
- d_keys: bfloat16 [16384, 128], P(('shard', 'seq')), parts along dimension 0
- d_values: bfloat16 [16384, 128], P(('shard', 'seq')), parts along dimension 0
The draws below stay inside these ranges and needn't reach their ends.
There are 2 independent parts, one for each index of `shard`. The reference program is written for one: setup_inputs(seed, part) draws one part's arguments, and reference() takes and returns one part's arrays. A program takes and returns all parts, laid end to end along the dimension named above; each array names one. Nothing has to cross between parts.
Inputs may be any that keep to these rules, and one draw needn't show every extreme that they name: The 96 names of random_blocks in the rows of one device's 4 query blocks fall on at most 6 of them on any one device along seq, and on exactly 6 for some device.
All inputs are finite; a program needn't handle non-finite values.
Results may differ from the reference program's by a relative error of at most 0.035.
Values may be sent and summed in bfloat16 or wider, within the bound.
A program may use at most 128 MiB of HBM per device.

```python
import math
import jax
import jax.numpy as jnp
import numpy as np
from jax import lax

HD = 128
HQ = 8
BLK = 128
RAND = 3
G = 2
QB_DEV = 4
NB = 64
TOKENS = 8192
N_SEQ = 16


def drawn_pair(key):
    key_draw = jnp.clip(jax.random.normal(jax.random.fold_in(key, 11), (TOKENS, HD), jnp.float32), -4.0, 4.0)
    query_draw = jnp.clip(jax.random.normal(jax.random.fold_in(key, 12), (TOKENS, HQ * HD), jnp.float32), -4.0, 4.0)
    return (query_draw, key_draw)


def draw_queries(key, part):
    return drawn_pair(key)[0].astype(jnp.bfloat16)


def draw_key_rows(key, part):
    return drawn_pair(key)[1].astype(jnp.bfloat16)


def draw_random_blocks(key, part):
    pick_count = QB_DEV * HQ * RAND

    def one_device(device_key):
        owner_order = jax.random.permutation(jax.random.fold_in(device_key, 1), N_SEQ)
        shuffle = jax.random.permutation(jax.random.fold_in(device_key, 2), pick_count)
        owners = owner_order[shuffle % N_SEQ]
        local_ids = jax.random.randint(jax.random.fold_in(device_key, 3), (pick_count,), 0, QB_DEV)
        return (owners * QB_DEV + local_ids).reshape(QB_DEV, HQ, RAND)
    device_keys = jax.random.split(jax.random.fold_in(key, 7), N_SEQ)
    return jax.vmap(one_device)(device_keys).reshape(NB, HQ, RAND).astype(jnp.int32)


def levels(stream_key, dims, cuts, smallest, largest):
    def one(axis_at, parts):
        heights = jax.random.uniform(jax.random.fold_in(jax.random.fold_in(stream_key, 6), axis_at), (parts,), jnp.float32, smallest / len(cuts), largest / len(cuts))
        return jnp.repeat(jnp.exp(heights), dims[axis_at] // parts).reshape((-1,) + (1,) * (len(dims) - axis_at - 1))

    level = one(*cuts[0])
    for cut in cuts[1:]:
        level = level * one(*cut)
    return level


def profile(number_of, total, reach, skew):
    loads = [(1 << 20) // math.isqrt(rank ** skew) + 1 for rank in range(2, number_of + 1)]
    rest, given = total - reach - (number_of - 1), [1] * (number_of - 1)
    while rest > 0:
        candidates = [i for i in range(number_of - 1) if given[i] < reach]
        whole, remaining = sum([loads[i] for i in candidates]), rest
        for i in candidates:
            extra = min(reach - given[i], max(1, remaining * loads[i] // whole), rest)
            given[i] = given[i] + extra
            rest = rest - extra
    return np.array([reach] + given)


def uneven(own_key, number_of, total, reach, lean):
    if number_of == 2:
        one = jax.random.randint(own_key, (), max(1, total - reach), min(reach, total - 1) + 1)
        return jnp.stack([one, total - one])
    lengths = jnp.asarray(profile(number_of, total, reach, lean), jnp.int32)
    twos = (number_of - 1) // 2
    giver, sink = lengths[1:1 + 2 * twos:2], lengths[2:2 + 2 * twos:2]
    slack = jnp.minimum(giver - 1, reach - sink)
    moved = jax.random.randint(jax.random.fold_in(own_key, 1), (twos,), 0, 1 << 20) % (slack + 1)
    lengths = lengths.at[1:1 + 2 * twos:2].set(giver - moved).at[2:2 + 2 * twos:2].set(sink + moved)
    return lengths[jax.random.permutation(jax.random.fold_in(own_key, 2), number_of)]


def scatter_about(stream_key, shape, spread, bound, cuts=(), kind=jnp.bfloat16):
    values = jax.random.normal(stream_key, shape, jnp.float32) * spread
    if len(cuts) > 0:
        values = levels(stream_key, shape, cuts, -0.22, 0.18) * values
    return jnp.clip(values, min=-bound, max=bound).astype(kind)


def setup_inputs(seed: int = 0, part: int = 0) -> dict:
    arg_keys = jax.random.split(jax.random.key(seed), 8)
    part_splits = jax.random.split(jax.random.fold_in(arg_keys[7], part), 8)
    return {
        "queries": draw_queries(jax.random.fold_in(jax.random.fold_in(arg_keys[7], part), 71), part),
        "key_rows": draw_key_rows(jax.random.fold_in(jax.random.fold_in(arg_keys[7], part), 71), part),
        "value_rows": scatter_about(part_splits[2], (TOKENS, HD), 1.0, 6.0, ((0, 16),)),
        "out_grads": scatter_about(part_splits[3], (TOKENS, HQ * HD), 1.0, 6.0, ((0, 16),)),
        "segment_ids": jnp.searchsorted(jnp.cumsum(uneven(part_splits[4], 2, TOKENS, TOKENS - TOKENS // 8, 0)), jnp.arange(TOKENS), side="right").astype(jnp.int32),
        "random_blocks": draw_random_blocks(jax.random.fold_in(jax.random.fold_in(arg_keys[7], part), 71), part),
        "global_blocks": jax.random.randint(part_splits[6], (G,), 0, NB).astype(jnp.int32),
    }


masked_value = -1e+30

def block_pass(query_block, grad_block, shared, shared_live, query_segs, shared_segs, random_kv, random_segs, scaling):
    query_wide = query_block.astype(jnp.float32)
    grad_wide = grad_block.astype(jnp.float32)
    shared_wide = shared.astype(jnp.float32)
    random_wide = random_kv.astype(jnp.float32)
    shared_mask = (query_segs[:, None, None] == shared_segs[None]) & shared_live[None, :, None]
    random_mask = query_segs[None, :, None, None] == random_segs[:, None]
    shared_scores = jnp.einsum('thd,jkd->htjk', query_wide, shared_wide[:, :, :HD]) * scaling
    shared_scores = jnp.where(shared_mask[None], shared_scores, masked_value)
    random_scores = jnp.einsum('thd,hrkd->htrk', query_wide, random_wide[:, :, :, :HD]) * scaling
    random_scores = jnp.where(random_mask, random_scores, masked_value)
    top_score = jnp.maximum(lax.optimization_barrier(jnp.max(shared_scores, axis=(2, 3))), lax.optimization_barrier(jnp.max(random_scores, axis=(2, 3))))
    totals = lax.optimization_barrier(jnp.sum(jnp.exp(shared_scores - top_score[:, :, None, None]), axis=(2, 3)))
    totals = totals + lax.optimization_barrier(jnp.sum(jnp.exp(random_scores - top_score[:, :, None, None]), axis=(2, 3)))
    log_totals = top_score + jnp.log(totals)
    shared_probs = jnp.exp(shared_scores - log_totals[:, :, None, None])
    random_probs = jnp.exp(random_scores - log_totals[:, :, None, None])
    shared_half = shared_probs.astype(jnp.bfloat16).astype(jnp.float32)
    random_half = random_probs.astype(jnp.bfloat16).astype(jnp.float32)
    attended = jnp.einsum('htjk,jkd->thd', shared_half, shared_wide[:, :, HD:])
    attended = (attended + jnp.einsum('htrk,hrkd->thd', random_half, random_wide[:, :, :, HD:])).astype(jnp.bfloat16)
    row_dots = jnp.einsum('thd,thd->ht', grad_wide, attended.astype(jnp.float32))
    shared_dprobs = jnp.einsum('thd,jkd->htjk', grad_wide, shared_wide[:, :, HD:])
    random_dprobs = jnp.einsum('thd,hrkd->htrk', grad_wide, random_wide[:, :, :, HD:])
    shared_dscores = (shared_probs * (shared_dprobs - row_dots[:, :, None, None])).astype(jnp.bfloat16).astype(jnp.float32)
    random_dscores = (random_probs * (random_dprobs - row_dots[:, :, None, None])).astype(jnp.bfloat16).astype(jnp.float32)
    query_grads = jnp.einsum('htjk,jkd->thd', shared_dscores, shared_wide[:, :, :HD])
    query_grads = query_grads + jnp.einsum('htrk,hrkd->thd', random_dscores, random_wide[:, :, :, :HD])
    query_grads = (query_grads * scaling).astype(jnp.bfloat16)
    shared_kgrad = jnp.einsum('htjk,thd->jkd', shared_dscores, query_wide) * scaling
    shared_vgrad = jnp.einsum('htjk,thd->jkd', shared_half, grad_wide)
    shared_grads = jnp.where(shared_live[:, None, None], jnp.concatenate([shared_kgrad, shared_vgrad], axis=2), 0.0)
    random_kgrad = jnp.einsum('htrk,thd->hrkd', random_dscores, query_wide) * scaling
    random_vgrad = jnp.einsum('htrk,thd->hrkd', random_half, grad_wide)
    random_grads = jnp.concatenate([random_kgrad, random_vgrad], axis=3)
    return (attended, query_grads, shared_grads, random_grads)

def reference(queries, key_rows, value_rows, out_grads, segment_ids, random_blocks, global_blocks):
    scaling = 1.0 / math.sqrt(HD)
    joined = jnp.concatenate([key_rows, value_rows], axis=1).reshape(NB, BLK, 2 * HD)
    seg_blocks = segment_ids.reshape(NB, BLK)
    query_blocks = queries.reshape(NB, BLK, HQ, HD)
    grad_blocks = out_grads.reshape(NB, BLK, HQ, HD)
    global_ids = global_blocks.astype(jnp.int32)

    def advance(gradients, block_index):
        window_ids = block_index + jnp.arange(-1, 2, dtype=jnp.int32)
        window_live = (window_ids >= 0) & (window_ids < NB)
        shared_ids = jnp.concatenate([jnp.clip(window_ids, 0, NB - 1), global_ids])
        shared_live = jnp.concatenate([window_live, jnp.ones((G,), bool)])
        random_ids = random_blocks[block_index].astype(jnp.int32)
        attended, query_grads, shared_grads, random_grads = block_pass(query_blocks[block_index], grad_blocks[block_index], joined[shared_ids], shared_live, seg_blocks[block_index], seg_blocks[shared_ids], joined[random_ids], seg_blocks[random_ids], scaling)
        gradients = gradients.at[shared_ids].add(shared_grads)
        gradients = gradients.at[random_ids.reshape(-1)].add(random_grads.reshape(HQ * RAND, BLK, 2 * HD))
        return (gradients, (attended, query_grads))
    start_grads = jnp.zeros((NB, BLK, 2 * HD), jnp.float32)
    gradients, (attended, query_grads) = lax.scan(advance, start_grads, jnp.arange(NB, dtype=jnp.int32))
    flat_grads = gradients.reshape(TOKENS, 2 * HD)
    return (attended.reshape(TOKENS, HQ * HD), query_grads.reshape(TOKENS, HQ * HD), flat_grads[:, :HD].astype(jnp.bfloat16), flat_grads[:, HD:].astype(jnp.bfloat16))
```

```python
import math

import jax
import jax.numpy as jnp
from jax import lax
from jax.experimental import pallas as pl
from jax.experimental.pallas import tpu as pltpu
from jax.sharding import PartitionSpec as P

HD = 128
HQ = 8
BLK = 128
RAND = 3
G = 2


masked_value = -1e30


def with_halo(array, sides, width):
    for axis, dim in sides:
        size, length = (lax.axis_size(axis), array.shape[dim])
        up = [(i, (i + 1) % size) for i in range(size - 1)]
        down = [(j, i) for i, j in up]
        last = lax.slice_in_dim(array, length - width, length, axis=dim)
        first = lax.slice_in_dim(array, 0, width, axis=dim)
        before = lax.ppermute(last, axis, up)
        after = lax.ppermute(first, axis, down)
        array = jnp.concatenate([before, array, after], axis=dim)
    return array


def spread(block, axis, owner):
    block = jnp.where(lax.axis_index(axis) == owner, block, jnp.zeros_like(block))
    return lax.psum(block, axis)


def from_behind(block, axis, distance):
    devices = range(lax.axis_size(axis))
    route = [(i - distance, i) for i in devices if i - distance in devices]
    return lax.ppermute(block, axis, route)


def routing(block_ids, per_device):
    owners = block_ids // per_device
    ordering = jnp.arange(block_ids.shape[0])
    earlier = (owners[:, None] == owners[None, :]) & (ordering[None, :] < ordering[:, None])
    return (owners, jnp.sum(earlier.astype(jnp.int32), axis=1))


def block_pass(
    query_block,
    grad_block,
    shared,
    shared_live,
    query_segs,
    shared_segs,
    random_kv,
    random_segs,
    scaling,
):
    wide = jnp.float32
    shared_mask = (query_segs[:, None, None] == shared_segs[None]) & shared_live[None, :, None]
    random_mask = query_segs[None, :, None, None] == random_segs[:, None]
    shared_scores = (
        jnp.einsum("thd,jkd->htjk", query_block, shared[:, :, :HD], preferred_element_type=wide)
        * scaling
    )
    shared_scores = jnp.where(shared_mask[None], shared_scores, masked_value)
    random_scores = (
        jnp.einsum(
            "thd,hrkd->htrk", query_block, random_kv[:, :, :, :HD], preferred_element_type=wide
        )
        * scaling
    )
    random_scores = jnp.where(random_mask, random_scores, masked_value)
    top_score = jnp.maximum(
        jnp.max(shared_scores, axis=(2, 3)), jnp.max(random_scores, axis=(2, 3))
    )
    totals = jnp.sum(jnp.exp(shared_scores - top_score[:, :, None, None]), axis=(2, 3))
    totals = totals + jnp.sum(jnp.exp(random_scores - top_score[:, :, None, None]), axis=(2, 3))
    log_totals = top_score + jnp.log(totals)
    shared_probs = jnp.exp(shared_scores - log_totals[:, :, None, None])
    random_probs = jnp.exp(random_scores - log_totals[:, :, None, None])
    shared_half = shared_probs.astype(jnp.bfloat16)
    random_half = random_probs.astype(jnp.bfloat16)
    attended = jnp.einsum(
        "htjk,jkd->thd", shared_half, shared[:, :, HD:], preferred_element_type=wide
    )
    attended = attended + jnp.einsum(
        "htrk,hrkd->thd", random_half, random_kv[:, :, :, HD:], preferred_element_type=wide
    )
    attended = attended.astype(jnp.bfloat16)
    row_dots = jnp.einsum("thd,thd->ht", grad_block, attended, preferred_element_type=wide)
    shared_dprobs = jnp.einsum(
        "thd,jkd->htjk", grad_block, shared[:, :, HD:], preferred_element_type=wide
    )
    random_dprobs = jnp.einsum(
        "thd,hrkd->htrk", grad_block, random_kv[:, :, :, HD:], preferred_element_type=wide
    )
    shared_dscores = (shared_probs * (shared_dprobs - row_dots[:, :, None, None])).astype(
        jnp.bfloat16
    )
    random_dscores = (random_probs * (random_dprobs - row_dots[:, :, None, None])).astype(
        jnp.bfloat16
    )
    query_grads = jnp.einsum(
        "htjk,jkd->thd", shared_dscores, shared[:, :, :HD], preferred_element_type=wide
    )
    query_grads = query_grads + jnp.einsum(
        "htrk,hrkd->thd", random_dscores, random_kv[:, :, :, :HD], preferred_element_type=wide
    )
    query_grads = (query_grads * scaling).astype(jnp.bfloat16)
    shared_kgrad = (
        jnp.einsum("htjk,thd->jkd", shared_dscores, query_block, preferred_element_type=wide)
        * scaling
    )
    shared_vgrad = jnp.einsum("htjk,thd->jkd", shared_half, grad_block, preferred_element_type=wide)
    shared_grads = jnp.where(
        shared_live[:, None, None], jnp.concatenate([shared_kgrad, shared_vgrad], axis=2), 0.0
    )
    random_kgrad = (
        jnp.einsum("htrk,thd->hrkd", random_dscores, query_block, preferred_element_type=wide)
        * scaling
    )
    random_vgrad = jnp.einsum(
        "htrk,thd->hrkd", random_half, grad_block, preferred_element_type=wide
    )
    random_grads = jnp.concatenate([random_kgrad, random_vgrad], axis=3)
    return (attended, query_grads, shared_grads, random_grads, log_totals, row_dots)


def body(queries, key_rows, value_rows, out_grads, segment_ids, random_blocks, global_blocks):
    scaling = 1.0 / math.sqrt(HD)
    row_count = queries.shape[0]
    qcount = row_count // BLK
    devices = lax.axis_size("seq")
    position = lax.axis_index("seq")
    total_blocks = segment_ids.shape[0] // BLK
    seg_blocks = segment_ids.reshape(total_blocks, BLK)
    joined = jnp.concatenate([key_rows, value_rows], axis=1)
    local_blocks = joined.reshape(qcount, BLK, 2 * HD)
    padded = with_halo(joined, (("seq", 0),), BLK)
    owned = global_blocks // qcount == position
    pieces = []
    for global_slot in range(G):
        picked = lax.dynamic_index_in_dim(
            local_blocks, global_blocks[global_slot] % qcount, 0, keepdims=False
        )
        pieces.append(spread(picked, "seq", global_blocks[global_slot] // qcount))
    global_kv = jnp.stack(pieces)
    chosen_ids = random_blocks.reshape(-1)
    pick_count = chosen_ids.shape[0]
    capacity = -(-pick_count // devices)
    owners, slots = routing(chosen_ids, qcount)
    outgoing_ids = (
        jnp.full((devices, capacity), -1, jnp.int32).at[owners, slots].set(chosen_ids % qcount)
    )
    wanted = lax.all_to_all(outgoing_ids, "seq", split_axis=0, concat_axis=0, tiled=True)
    wanted_clip = jnp.clip(wanted, 0, qcount - 1)
    served = local_blocks[wanted_clip]
    answer = lax.all_to_all(served, "seq", split_axis=0, concat_axis=0, tiled=True)
    random_kv = answer[owners, slots].reshape(qcount, HQ, RAND, BLK, 2 * HD)
    query_blocks = queries.reshape(qcount, BLK, HQ, HD)
    grad_blocks = out_grads.reshape(qcount, BLK, HQ, HD)

    def attend(bundle):
        block_index, query_block, grad_block, block_kv, block_ids = bundle
        global_index = position * qcount + block_index
        window = lax.dynamic_slice_in_dim(padded, block_index * BLK, 3 * BLK, 0).reshape(
            3, BLK, 2 * HD
        )
        window_ids = global_index + jnp.arange(-1, 2, dtype=jnp.int32)
        window_live = (window_ids >= 0) & (window_ids < total_blocks)
        shared_ids = jnp.concatenate([jnp.clip(window_ids, 0, total_blocks - 1), global_blocks])
        shared_live = jnp.concatenate([window_live, jnp.ones((G,), bool)])
        shared = jnp.concatenate([window, global_kv], axis=0)
        return block_pass(
            query_block,
            grad_block,
            shared,
            shared_live,
            seg_blocks[global_index],
            seg_blocks[shared_ids],
            block_kv,
            seg_blocks[block_ids],
            scaling,
        )

    attended, query_grads, shared_grads, random_grads, log_totals, row_dots = lax.map(
        attend,
        (jnp.arange(qcount, dtype=jnp.int32), query_blocks, grad_blocks, random_kv, random_blocks),
    )
    window_sum = jnp.zeros((qcount + 2, BLK, 2 * HD), jnp.float32)
    for offset in range(3):
        window_sum = window_sum.at[offset : offset + qcount].add(shared_grads[:, offset])
    from_right = from_behind(window_sum[0].astype(jnp.bfloat16), "seq", -1).astype(jnp.float32)
    from_left = from_behind(window_sum[qcount + 1].astype(jnp.bfloat16), "seq", 1).astype(
        jnp.float32
    )
    own_grads = window_sum[1 : qcount + 1]
    own_grads = own_grads.at[qcount - 1].add(from_right).at[0].add(from_left)
    global_sum = lax.psum(jnp.sum(shared_grads[:, 3:], axis=0), "seq")
    global_hits = (
        (global_blocks[:, None] % qcount == jnp.arange(qcount)[None, :]) & owned[:, None]
    ).astype(jnp.float32)
    own_grads = own_grads + jnp.einsum(
        "gq,gkd->qkd", global_hits, global_sum, precision=lax.Precision.HIGHEST
    )
    outgoing = (
        jnp.zeros((devices, capacity, BLK, 2 * HD), jnp.float32)
        .at[owners, slots]
        .set(random_grads.reshape(pick_count, BLK, 2 * HD))
    )
    returned = lax.all_to_all(outgoing, "seq", split_axis=0, concat_axis=0, tiled=True)
    request_hits = (wanted[:, :, None] == jnp.arange(qcount)[None, None, :]).astype(jnp.float32)
    own_grads = own_grads + jnp.einsum(
        "ncq,nckd->qkd", request_hits, returned, precision=lax.Precision.HIGHEST
    )
    own_flat = own_grads.reshape(row_count, 2 * HD)
    return (
        attended.reshape(row_count, HQ * HD),
        query_grads.reshape(row_count, HQ * HD),
        own_flat[:, :HD].astype(jnp.bfloat16),
        own_flat[:, HD:].astype(jnp.bfloat16),
    )


SUM_TYPE = jnp.float32
HEADS_STEP = 2
LOG2E = 1.4426950408889634
DENSE_BYTES = 16 * 1024 * 1024


def attention_kernel(
    meta_ref,
    random_ref,
    global_ref,
    query_ref,
    grad_ref,
    kv_ref,
    attended_ref,
    query_grad_ref,
    sums_ref,
    kvt_ref,
    acc_ref,
    shared_acc_ref,
):
    wide = jnp.float32
    half = jnp.bfloat16
    block = pl.program_id(0)
    group = pl.program_id(1)
    groups = pl.num_programs(1)
    total_blocks = kv_ref.shape[0]
    heads = query_ref.shape[1] // HD
    scaling = 1.0 / math.sqrt(HD)
    boundary = meta_ref[0]
    mine = meta_ref[1] + block

    @pl.when((block == 0) & (group == 0))
    def _():
        @pl.loop(0, total_blocks)
        def _(index):
            kvt_ref[index] = kv_ref[index].T
            acc_ref[index] = jnp.zeros((BLK, 2 * HD), wide)

    @pl.when(group == 0)
    def _():
        shared_acc_ref[...] = jnp.zeros(shared_acc_ref.shape, wide)

    shared_ids = [
        jnp.maximum(mine - 1, 0),
        mine,
        jnp.minimum(mine + 1, total_blocks - 1),
        global_ref[0],
        global_ref[1],
    ]
    dead = [
        jnp.where(mine == 0, masked_value, 0.0).astype(wide),
        None,
        jnp.where(mine == total_blocks - 1, masked_value, 0.0).astype(wide),
        None,
        None,
    ]
    random_ids = [
        [random_ref[(block * groups + group) * heads * RAND + head * RAND + pick] for head in range(heads)]
        for pick in range(RAND)
    ]

    queries = [query_ref[:, head * HD : (head + 1) * HD] for head in range(heads)]
    grads = [grad_ref[:, head * HD : (head + 1) * HD] for head in range(heads)]
    query_stack = jnp.concatenate(queries, axis=0)
    grad_stack = jnp.concatenate(grads, axis=0)

    def against(rows, columns):
        return lax.dot_general(rows, columns, (((1,), (1,)), ((), ())), preferred_element_type=wide)

    def product(rows, columns):
        return jnp.dot(rows, columns, preferred_element_type=wide)

    def entries(start, stack, parts):
        tiles = [against(kv_ref[i, :, start : start + HD], stack) for i in shared_ids]
        for names in random_ids:
            tiles.append(
                jnp.concatenate(
                    [
                        against(kv_ref[i, :, start : start + HD], part)
                        for i, part in zip(names, parts)
                    ],
                    axis=1,
                )
            )
        return tiles

    key_row = lax.broadcasted_iota(jnp.int32, (BLK, HD), 0)
    query_low = lax.broadcasted_iota(jnp.int32, (BLK, HD), 1) < boundary - mine * BLK

    def allowed(name):
        return (key_row < boundary - name * BLK) == query_low

    scores = entries(0, query_stack, queries)
    factor = scaling * LOG2E
    masked = []
    for slot, tile in enumerate(scores):
        pieces = []
        for head in range(heads):
            piece = tile[:, head * BLK : (head + 1) * BLK] * factor
            name = shared_ids[slot] if slot < 5 else random_ids[slot - 5][head]
            piece = jnp.where(allowed(name), piece, masked_value)
            if slot < 5 and dead[slot] is not None:
                piece = piece + dead[slot]
            pieces.append(piece)
        masked.append(jnp.concatenate(pieces, axis=1))
    top = masked[0]
    for tile in masked[1:]:
        top = jnp.maximum(top, tile)
    top = jnp.max(top, axis=0, keepdims=True)
    powers = [jnp.exp2(tile - top) for tile in masked]
    total = powers[0]
    for tile in powers[1:]:
        total = total + tile
    inverse = 1.0 / jnp.sum(total, axis=0, keepdims=True)
    probs = [tile * inverse for tile in powers]
    probs_half = [tile.astype(half) for tile in probs]

    def gathered(start, tiles):
        shared = product(
            jnp.concatenate([kvt_ref[i, start : start + HD, :] for i in shared_ids], axis=1),
            jnp.concatenate(tiles[:5], axis=0),
        )
        pieces = []
        for head in range(heads):
            names = [random_ids[pick][head] for pick in range(RAND)]
            pieces.append(
                product(
                    jnp.concatenate([kvt_ref[i, start : start + HD, :] for i in names], axis=1),
                    jnp.concatenate(
                        [tile[:, head * BLK : (head + 1) * BLK] for tile in tiles[5:]], axis=0
                    ),
                )
            )
        return shared + jnp.concatenate(pieces, axis=1)

    attended = gathered(HD, probs_half).astype(half).astype(wide)
    grads_turned = jnp.concatenate([part.astype(wide).T for part in grads], axis=1)
    row_dots = jnp.sum(attended * grads_turned, axis=0, keepdims=True)
    for head in range(heads):
        span = slice(head * BLK, (head + 1) * BLK)
        attended_ref[:, span] = attended[:, span].T.astype(half)
    dprobs = entries(HD, grad_stack, grads)
    dscores = [(p * (d - row_dots)).astype(half) for p, d in zip(probs, dprobs)]
    query_grads = gathered(0, dscores) * scaling
    for head in range(heads):
        span = slice(head * BLK, (head + 1) * BLK)
        query_grad_ref[:, span] = query_grads[:, span].T.astype(half)
    for slot in range(5):
        shared_acc_ref[slot, :, :HD] += product(dscores[slot], query_stack)
        shared_acc_ref[slot, :, HD:] += product(probs_half[slot], grad_stack)
    for pick in range(RAND):
        for head in range(heads):
            name = random_ids[pick][head]
            span = slice(head * BLK, (head + 1) * BLK)
            acc_ref[name, :, :HD] += product(dscores[5 + pick][:, span], queries[head])
            acc_ref[name, :, HD:] += product(probs_half[5 + pick][:, span], grads[head])

    @pl.when(group == groups - 1)
    def _():
        for slot in range(5):
            acc_ref[shared_ids[slot]] += shared_acc_ref[slot]

    @pl.when((block == pl.num_programs(0) - 1) & (group == groups - 1))
    def _():
        @pl.loop(0, total_blocks)
        def _(index):
            sums_ref[index, :, :HD] = (acc_ref[index, :, :HD] * scaling).astype(sums_ref.dtype)
            sums_ref[index, :, HD:] = acc_ref[index, :, HD:].astype(sums_ref.dtype)


def attention_call(meta, random_ids, global_ids, queries, out_grads, kv):
    row_count = queries.shape[0]
    total_blocks = kv.shape[0]
    width = HEADS_STEP * HD
    rows = pl.BlockSpec((BLK, width), lambda b, g, *_: (b, g))
    whole = pl.BlockSpec((total_blocks, BLK, 2 * HD), lambda b, g, *_: (0, 0, 0))
    return pl.pallas_call(
        attention_kernel,
        grid_spec=pltpu.PrefetchScalarGridSpec(
            num_scalar_prefetch=3,
            grid=(row_count // BLK, HQ // HEADS_STEP),
            in_specs=[rows, rows, whole],
            out_specs=[rows, rows, whole],
            scratch_shapes=[
                pltpu.VMEM((total_blocks, 2 * HD, BLK), jnp.bfloat16),
                pltpu.VMEM((total_blocks, BLK, 2 * HD), jnp.float32),
                pltpu.VMEM((5, BLK, 2 * HD), jnp.float32),
            ],
        ),
        out_shape=[
            jax.ShapeDtypeStruct(queries.shape, jnp.bfloat16),
            jax.ShapeDtypeStruct(queries.shape, jnp.bfloat16),
            jax.ShapeDtypeStruct(kv.shape, SUM_TYPE),
        ],
        compiler_params=pltpu.CompilerParams(
            dimension_semantics=("arbitrary", "arbitrary"),
            vmem_limit_bytes=56 * 1024 * 1024,
        ),
        name="block_attention",
    )(meta, random_ids, global_ids, queries, out_grads, kv)


def dense_body(queries, key_rows, value_rows, out_grads, segment_ids, random_blocks, global_blocks):
    qcount = queries.shape[0] // BLK
    position = lax.axis_index("seq")
    total_blocks = segment_ids.shape[0] // BLK
    joined = jnp.concatenate([key_rows, value_rows], axis=1)
    kv = lax.all_gather(joined, "seq", axis=0, tiled=True).reshape(total_blocks, BLK, 2 * HD)
    boundary = jnp.sum((segment_ids == segment_ids[0]).astype(jnp.int32))
    meta = jnp.stack([boundary, (position * qcount).astype(jnp.int32)])
    attended, query_grads, sums = attention_call(
        meta, random_blocks.reshape(-1), global_blocks, queries, out_grads, kv
    )
    own = lax.psum_scatter(
        sums.reshape(total_blocks * BLK, 2 * HD), "seq", scatter_dimension=0, tiled=True
    )
    return (
        attended,
        query_grads,
        own[:, :HD].astype(jnp.bfloat16),
        own[:, HD:].astype(jnp.bfloat16),
    )


def plan(*arrays):
    tokens = arrays[4].shape[0]
    chosen = dense_body if tokens * 2 * HD * 4 <= DENSE_BYTES else body
    return chosen(*arrays)


def solution(mesh):
    placed = (
        P(("shard", "seq"), None),
        P(("shard", "seq"), None),
        P(("shard", "seq"), None),
        P(("shard", "seq"), None),
        P("shard"),
        P(("shard", "seq"), None, None),
        P("shard"),
    )
    return jax.shard_map(
        plan,
        mesh=mesh,
        in_specs=placed,
        out_specs=(
            P(("shard", "seq"), None),
            P(("shard", "seq"), None),
            P(("shard", "seq"), None),
            P(("shard", "seq"), None),
        ),
        check_vma=False,
    )
```

```python
import math

import jax
import jax.numpy as jnp
from jax import lax
from jax.experimental import pallas as pl
from jax.experimental.pallas import tpu as pltpu
from jax.sharding import PartitionSpec as P

HD = 128
HQ = 8
BLK = 128
RAND = 3
G = 2


masked_value = -1e30


def with_halo(array, sides, width):
    for axis, dim in sides:
        size, length = (lax.axis_size(axis), array.shape[dim])
        up = [(i, (i + 1) % size) for i in range(size - 1)]
        down = [(j, i) for i, j in up]
        last = lax.slice_in_dim(array, length - width, length, axis=dim)
        first = lax.slice_in_dim(array, 0, width, axis=dim)
        before = lax.ppermute(last, axis, up)
        after = lax.ppermute(first, axis, down)
        array = jnp.concatenate([before, array, after], axis=dim)
    return array


def spread(block, axis, owner):
    block = jnp.where(lax.axis_index(axis) == owner, block, jnp.zeros_like(block))
    return lax.psum(block, axis)


def from_behind(block, axis, distance):
    devices = range(lax.axis_size(axis))
    route = [(i - distance, i) for i in devices if i - distance in devices]
    return lax.ppermute(block, axis, route)


def routing(block_ids, per_device):
    owners = block_ids // per_device
    ordering = jnp.arange(block_ids.shape[0])
    earlier = (owners[:, None] == owners[None, :]) & (ordering[None, :] < ordering[:, None])
    return (owners, jnp.sum(earlier.astype(jnp.int32), axis=1))


def block_pass(
    query_block,
    grad_block,
    shared,
    shared_live,
    query_segs,
    shared_segs,
    random_kv,
    random_segs,
    scaling,
):
    wide = jnp.float32
    shared_mask = (query_segs[:, None, None] == shared_segs[None]) & shared_live[None, :, None]
    random_mask = query_segs[None, :, None, None] == random_segs[:, None]
    shared_scores = (
        jnp.einsum("thd,jkd->htjk", query_block, shared[:, :, :HD], preferred_element_type=wide)
        * scaling
    )
    shared_scores = jnp.where(shared_mask[None], shared_scores, masked_value)
    random_scores = (
        jnp.einsum(
            "thd,hrkd->htrk", query_block, random_kv[:, :, :, :HD], preferred_element_type=wide
        )
        * scaling
    )
    random_scores = jnp.where(random_mask, random_scores, masked_value)
    top_score = jnp.maximum(
        jnp.max(shared_scores, axis=(2, 3)), jnp.max(random_scores, axis=(2, 3))
    )
    totals = jnp.sum(jnp.exp(shared_scores - top_score[:, :, None, None]), axis=(2, 3))
    totals = totals + jnp.sum(jnp.exp(random_scores - top_score[:, :, None, None]), axis=(2, 3))
    log_totals = top_score + jnp.log(totals)
    shared_probs = jnp.exp(shared_scores - log_totals[:, :, None, None])
    random_probs = jnp.exp(random_scores - log_totals[:, :, None, None])
    shared_half = shared_probs.astype(jnp.bfloat16)
    random_half = random_probs.astype(jnp.bfloat16)
    attended = jnp.einsum(
        "htjk,jkd->thd", shared_half, shared[:, :, HD:], preferred_element_type=wide
    )
    attended = attended + jnp.einsum(
        "htrk,hrkd->thd", random_half, random_kv[:, :, :, HD:], preferred_element_type=wide
    )
    attended = attended.astype(jnp.bfloat16)
    row_dots = jnp.einsum("thd,thd->ht", grad_block, attended, preferred_element_type=wide)
    shared_dprobs = jnp.einsum(
        "thd,jkd->htjk", grad_block, shared[:, :, HD:], preferred_element_type=wide
    )
    random_dprobs = jnp.einsum(
        "thd,hrkd->htrk", grad_block, random_kv[:, :, :, HD:], preferred_element_type=wide
    )
    shared_dscores = (shared_probs * (shared_dprobs - row_dots[:, :, None, None])).astype(
        jnp.bfloat16
    )
    random_dscores = (random_probs * (random_dprobs - row_dots[:, :, None, None])).astype(
        jnp.bfloat16
    )
    query_grads = jnp.einsum(
        "htjk,jkd->thd", shared_dscores, shared[:, :, :HD], preferred_element_type=wide
    )
    query_grads = query_grads + jnp.einsum(
        "htrk,hrkd->thd", random_dscores, random_kv[:, :, :, :HD], preferred_element_type=wide
    )
    query_grads = (query_grads * scaling).astype(jnp.bfloat16)
    shared_kgrad = (
        jnp.einsum("htjk,thd->jkd", shared_dscores, query_block, preferred_element_type=wide)
        * scaling
    )
    shared_vgrad = jnp.einsum("htjk,thd->jkd", shared_half, grad_block, preferred_element_type=wide)
    shared_grads = jnp.where(
        shared_live[:, None, None], jnp.concatenate([shared_kgrad, shared_vgrad], axis=2), 0.0
    )
    random_kgrad = (
        jnp.einsum("htrk,thd->hrkd", random_dscores, query_block, preferred_element_type=wide)
        * scaling
    )
    random_vgrad = jnp.einsum(
        "htrk,thd->hrkd", random_half, grad_block, preferred_element_type=wide
    )
    random_grads = jnp.concatenate([random_kgrad, random_vgrad], axis=3)
    return (attended, query_grads, shared_grads, random_grads, log_totals, row_dots)


def body(queries, key_rows, value_rows, out_grads, segment_ids, random_blocks, global_blocks):
    scaling = 1.0 / math.sqrt(HD)
    row_count = queries.shape[0]
    qcount = row_count // BLK
    devices = lax.axis_size("seq")
    position = lax.axis_index("seq")
    total_blocks = segment_ids.shape[0] // BLK
    seg_blocks = segment_ids.reshape(total_blocks, BLK)
    joined = jnp.concatenate([key_rows, value_rows], axis=1)
    local_blocks = joined.reshape(qcount, BLK, 2 * HD)
    padded = with_halo(joined, (("seq", 0),), BLK)
    owned = global_blocks // qcount == position
    pieces = []
    for global_slot in range(G):
        picked = lax.dynamic_index_in_dim(
            local_blocks, global_blocks[global_slot] % qcount, 0, keepdims=False
        )
        pieces.append(spread(picked, "seq", global_blocks[global_slot] // qcount))
    global_kv = jnp.stack(pieces)
    chosen_ids = random_blocks.reshape(-1)
    pick_count = chosen_ids.shape[0]
    capacity = -(-pick_count // devices)
    owners, slots = routing(chosen_ids, qcount)
    outgoing_ids = (
        jnp.full((devices, capacity), -1, jnp.int32).at[owners, slots].set(chosen_ids % qcount)
    )
    wanted = lax.all_to_all(outgoing_ids, "seq", split_axis=0, concat_axis=0, tiled=True)
    wanted_clip = jnp.clip(wanted, 0, qcount - 1)
    served = local_blocks[wanted_clip]
    answer = lax.all_to_all(served, "seq", split_axis=0, concat_axis=0, tiled=True)
    random_kv = answer[owners, slots].reshape(qcount, HQ, RAND, BLK, 2 * HD)
    query_blocks = queries.reshape(qcount, BLK, HQ, HD)
    grad_blocks = out_grads.reshape(qcount, BLK, HQ, HD)

    def attend(bundle):
        block_index, query_block, grad_block, block_kv, block_ids = bundle
        global_index = position * qcount + block_index
        window = lax.dynamic_slice_in_dim(padded, block_index * BLK, 3 * BLK, 0).reshape(
            3, BLK, 2 * HD
        )
        window_ids = global_index + jnp.arange(-1, 2, dtype=jnp.int32)
        window_live = (window_ids >= 0) & (window_ids < total_blocks)
        shared_ids = jnp.concatenate([jnp.clip(window_ids, 0, total_blocks - 1), global_blocks])
        shared_live = jnp.concatenate([window_live, jnp.ones((G,), bool)])
        shared = jnp.concatenate([window, global_kv], axis=0)
        return block_pass(
            query_block,
            grad_block,
            shared,
            shared_live,
            seg_blocks[global_index],
            seg_blocks[shared_ids],
            block_kv,
            seg_blocks[block_ids],
            scaling,
        )

    attended, query_grads, shared_grads, random_grads, log_totals, row_dots = lax.map(
        attend,
        (jnp.arange(qcount, dtype=jnp.int32), query_blocks, grad_blocks, random_kv, random_blocks),
    )
    window_sum = jnp.zeros((qcount + 2, BLK, 2 * HD), jnp.float32)
    for offset in range(3):
        window_sum = window_sum.at[offset : offset + qcount].add(shared_grads[:, offset])
    from_right = from_behind(window_sum[0].astype(jnp.bfloat16), "seq", -1).astype(jnp.float32)
    from_left = from_behind(window_sum[qcount + 1].astype(jnp.bfloat16), "seq", 1).astype(
        jnp.float32
    )
    own_grads = window_sum[1 : qcount + 1]
    own_grads = own_grads.at[qcount - 1].add(from_right).at[0].add(from_left)
    global_sum = lax.psum(jnp.sum(shared_grads[:, 3:], axis=0), "seq")
    global_hits = (
        (global_blocks[:, None] % qcount == jnp.arange(qcount)[None, :]) & owned[:, None]
    ).astype(jnp.float32)
    own_grads = own_grads + jnp.einsum(
        "gq,gkd->qkd", global_hits, global_sum, precision=lax.Precision.HIGHEST
    )
    outgoing = (
        jnp.zeros((devices, capacity, BLK, 2 * HD), jnp.float32)
        .at[owners, slots]
        .set(random_grads.reshape(pick_count, BLK, 2 * HD))
    )
    returned = lax.all_to_all(outgoing, "seq", split_axis=0, concat_axis=0, tiled=True)
    request_hits = (wanted[:, :, None] == jnp.arange(qcount)[None, None, :]).astype(jnp.float32)
    own_grads = own_grads + jnp.einsum(
        "ncq,nckd->qkd", request_hits, returned, precision=lax.Precision.HIGHEST
    )
    own_flat = own_grads.reshape(row_count, 2 * HD)
    return (
        attended.reshape(row_count, HQ * HD),
        query_grads.reshape(row_count, HQ * HD),
        own_flat[:, :HD].astype(jnp.bfloat16),
        own_flat[:, HD:].astype(jnp.bfloat16),
    )


SUM_TYPE = jnp.bfloat16
HEADS_STEP = 2
LOG2E = 1.4426950408889634
DENSE_BYTES = 16 * 1024 * 1024


def attention_kernel(
    meta_ref,
    random_ref,
    global_ref,
    query_ref,
    grad_ref,
    kv_ref,
    attended_ref,
    query_grad_ref,
    sums_ref,
    kvt_ref,
    acc_ref,
    shared_acc_ref,
):
    wide = jnp.float32
    half = jnp.bfloat16
    block = pl.program_id(0)
    group = pl.program_id(1)
    groups = pl.num_programs(1)
    total_blocks = kv_ref.shape[0]
    heads = query_ref.shape[1] // HD
    scaling = 1.0 / math.sqrt(HD)
    boundary = meta_ref[0]
    mine = meta_ref[1] + block

    @pl.when((block == 0) & (group == 0))
    def _():
        @pl.loop(0, total_blocks)
        def _(index):
            kvt_ref[index] = kv_ref[index].T
            acc_ref[index] = jnp.zeros((BLK, 2 * HD), wide)

    @pl.when(group == 0)
    def _():
        shared_acc_ref[...] = jnp.zeros(shared_acc_ref.shape, wide)

    shared_ids = [
        jnp.maximum(mine - 1, 0),
        mine,
        jnp.minimum(mine + 1, total_blocks - 1),
        global_ref[0],
        global_ref[1],
    ]
    dead = [
        jnp.where(mine == 0, masked_value, 0.0).astype(wide),
        None,
        jnp.where(mine == total_blocks - 1, masked_value, 0.0).astype(wide),
        None,
        None,
    ]
    random_ids = [
        [random_ref[(block * groups + group) * heads * RAND + head * RAND + pick] for head in range(heads)]
        for pick in range(RAND)
    ]

    queries = [query_ref[:, head * HD : (head + 1) * HD] for head in range(heads)]
    grads = [grad_ref[:, head * HD : (head + 1) * HD] for head in range(heads)]
    query_stack = jnp.concatenate(queries, axis=0)
    grad_stack = jnp.concatenate(grads, axis=0)

    def against(rows, columns):
        return lax.dot_general(rows, columns, (((1,), (1,)), ((), ())), preferred_element_type=wide)

    def product(rows, columns):
        return jnp.dot(rows, columns, preferred_element_type=wide)

    def entries(start, stack, parts):
        tiles = [against(kv_ref[i, :, start : start + HD], stack) for i in shared_ids]
        for names in random_ids:
            tiles.append(
                jnp.concatenate(
                    [
                        against(kv_ref[i, :, start : start + HD], part)
                        for i, part in zip(names, parts)
                    ],
                    axis=1,
                )
            )
        return tiles

    key_row = lax.broadcasted_iota(jnp.int32, (BLK, HD), 0)
    query_low = lax.broadcasted_iota(jnp.int32, (BLK, HD), 1) < boundary - mine * BLK

    def allowed(name):
        return (key_row < boundary - name * BLK) == query_low

    scores = entries(0, query_stack, queries)
    factor = scaling * LOG2E
    masked = []
    for slot, tile in enumerate(scores):
        pieces = []
        for head in range(heads):
            piece = tile[:, head * BLK : (head + 1) * BLK] * factor
            name = shared_ids[slot] if slot < 5 else random_ids[slot - 5][head]
            piece = jnp.where(allowed(name), piece, masked_value)
            if slot < 5 and dead[slot] is not None:
                piece = piece + dead[slot]
            pieces.append(piece)
        masked.append(jnp.concatenate(pieces, axis=1))
    top = masked[0]
    for tile in masked[1:]:
        top = jnp.maximum(top, tile)
    top = jnp.max(top, axis=0, keepdims=True)
    powers = [jnp.exp2(tile - top) for tile in masked]
    total = powers[0]
    for tile in powers[1:]:
        total = total + tile
    inverse = 1.0 / jnp.sum(total, axis=0, keepdims=True)
    probs = [tile * inverse for tile in powers]
    probs_half = [tile.astype(half) for tile in probs]

    def gathered(start, tiles):
        shared = product(
            jnp.concatenate([kvt_ref[i, start : start + HD, :] for i in shared_ids], axis=1),
            jnp.concatenate(tiles[:5], axis=0),
        )
        pieces = []
        for head in range(heads):
            names = [random_ids[pick][head] for pick in range(RAND)]
            pieces.append(
                product(
                    jnp.concatenate([kvt_ref[i, start : start + HD, :] for i in names], axis=1),
                    jnp.concatenate(
                        [tile[:, head * BLK : (head + 1) * BLK] for tile in tiles[5:]], axis=0
                    ),
                )
            )
        return shared + jnp.concatenate(pieces, axis=1)

    attended = gathered(HD, probs_half).astype(half).astype(wide)
    grads_turned = jnp.concatenate([part.astype(wide).T for part in grads], axis=1)
    row_dots = jnp.sum(attended * grads_turned, axis=0, keepdims=True)
    for head in range(heads):
        span = slice(head * BLK, (head + 1) * BLK)
        attended_ref[:, span] = attended[:, span].T.astype(half)
    dprobs = entries(HD, grad_stack, grads)
    dscores = [(p * (d - row_dots)).astype(half) for p, d in zip(probs, dprobs)]
    query_grads = gathered(0, dscores) * scaling
    for head in range(heads):
        span = slice(head * BLK, (head + 1) * BLK)
        query_grad_ref[:, span] = query_grads[:, span].T.astype(half)
    for slot in range(5):
        shared_acc_ref[slot, :, :HD] += product(dscores[slot], query_stack)
        shared_acc_ref[slot, :, HD:] += product(probs_half[slot], grad_stack)
    for pick in range(RAND):
        for head in range(heads):
            name = random_ids[pick][head]
            span = slice(head * BLK, (head + 1) * BLK)
            acc_ref[name, :, :HD] += product(dscores[5 + pick][:, span], queries[head])
            acc_ref[name, :, HD:] += product(probs_half[5 + pick][:, span], grads[head])

    @pl.when(group == groups - 1)
    def _():
        for slot in range(5):
            acc_ref[shared_ids[slot]] += shared_acc_ref[slot]

    @pl.when((block == pl.num_programs(0) - 1) & (group == groups - 1))
    def _():
        @pl.loop(0, total_blocks)
        def _(index):
            sums_ref[index, :, :HD] = (acc_ref[index, :, :HD] * scaling).astype(sums_ref.dtype)
            sums_ref[index, :, HD:] = acc_ref[index, :, HD:].astype(sums_ref.dtype)


def attention_call(meta, random_ids, global_ids, queries, out_grads, kv):
    row_count = queries.shape[0]
    total_blocks = kv.shape[0]
    width = HEADS_STEP * HD
    rows = pl.BlockSpec((BLK, width), lambda b, g, *_: (b, g))
    whole = pl.BlockSpec((total_blocks, BLK, 2 * HD), lambda b, g, *_: (0, 0, 0))
    return pl.pallas_call(
        attention_kernel,
        grid_spec=pltpu.PrefetchScalarGridSpec(
            num_scalar_prefetch=3,
            grid=(row_count // BLK, HQ // HEADS_STEP),
            in_specs=[rows, rows, whole],
            out_specs=[rows, rows, whole],
            scratch_shapes=[
                pltpu.VMEM((total_blocks, 2 * HD, BLK), jnp.bfloat16),
                pltpu.VMEM((total_blocks, BLK, 2 * HD), jnp.float32),
                pltpu.VMEM((5, BLK, 2 * HD), jnp.float32),
            ],
        ),
        out_shape=[
            jax.ShapeDtypeStruct(queries.shape, jnp.bfloat16),
            jax.ShapeDtypeStruct(queries.shape, jnp.bfloat16),
            jax.ShapeDtypeStruct(kv.shape, SUM_TYPE),
        ],
        compiler_params=pltpu.CompilerParams(
            dimension_semantics=("arbitrary", "arbitrary"),
            vmem_limit_bytes=56 * 1024 * 1024,
        ),
        name="block_attention",
    )(meta, random_ids, global_ids, queries, out_grads, kv)


LINE = 4
SEQ = 16


class Place:
    def __init__(self):
        me = lax.axis_index("seq")
        self.me = me
        self.core = lax.rem(me, 2)
        self.x = lax.rem(me // 2, 2)
        self.z = me // 4
        self.high = self.z // 2
        self.step = 1 - 2 * self.high
        self.inner = jnp.where((self.z == 1) | (self.z == 2), 1, 0)
        self.partner = self.at(self.z, self.x, 1 - self.core)
        self.across = self.at(self.z, 1 - self.x, self.core)
        self.onward = self.at(self.z + self.step, self.x, self.core)
        self.outward = self.at(self.z - self.step, self.x, self.core)

    def at(self, z, x, core):
        return z * 4 + x * 2 + core


def greet(place):
    barrier = pltpu.get_barrier_semaphore()
    for other in (place.partner, place.across, place.onward):
        pl.semaphore_signal(
            barrier, inc=1, device_id={"seq": other}, device_id_type=pl.DeviceIdType.MESH
        )

    @pl.when(place.inner == 1)
    def _():
        pl.semaphore_signal(
            barrier, inc=1, device_id={"seq": place.outward}, device_id_type=pl.DeviceIdType.MESH
        )

    pl.semaphore_wait(barrier, 3 + place.inner)


def remote(source, target, send, receive, device):
    return pltpu.make_async_remote_copy(
        src_ref=source,
        dst_ref=target,
        send_sem=send,
        recv_sem=receive,
        device_id={"seq": device},
        device_id_type=pl.DeviceIdType.MESH,
    )


def gather_kernel(key_ref, value_ref, out_ref, zs, zr, xs, xr, cs, cr):
    place = Place()
    z, step, inner = place.z, place.step, place.inner
    lines = [z, z + step - 2 * step * inner, z + step * (2 - inner), z + step * (3 - inner)]
    mine = [place.at(line, place.x, place.core) for line in lines]
    theirs = [place.at(line, 1 - place.x, place.core) for line in lines]
    out_ref[place.me, :, :HD] = key_ref[...]
    out_ref[place.me, :, HD:] = value_ref[...]
    greet(place)

    def send(slot, sends, index, receives, to, device):
        return remote(
            out_ref.at[slot], out_ref.at[slot], sends.at[index], receives.at[to], device
        )

    along = [send(mine[0], zs, 0, zr, 2, place.onward)]
    edge_own = send(mine[0], zs, 0, zr, 1, place.onward)
    out_own = send(mine[0], zs, 1, zr, 1, place.outward)
    relays = [
        send(mine[1], zs, 2, zr, 3, place.onward),
        send(mine[2], zs, 3, zr, 2, place.outward),
        send(mine[3], zs, 4, zr, 3, place.outward),
    ]
    arrivals = [
        send(mine[index], zs, 0, zr, index, place.onward) for index in range(1, LINE)
    ]
    crossing = [send(mine[k], xs, k, xr, k, place.across) for k in range(LINE)]
    crossed = [send(theirs[k], xs, k, xr, k, place.across) for k in range(LINE)]
    near = [send(mine[k], cs, k, cr, k, place.partner) for k in range(LINE)]
    far = [send(theirs[k], cs, LINE + k, cr, LINE + k, place.partner) for k in range(LINE)]

    @pl.when(inner == 0)
    def _():
        edge_own.start()

    @pl.when(inner == 1)
    def _():
        along[0].start()
        out_own.start()

    crossing[0].start()
    near[0].start()
    for k in range(1, LINE):
        arrivals[k - 1].wait_recv()

        @pl.when(inner == 1)
        def _(k=k):
            relays[k - 1].start()

        crossing[k].start()
        near[k].start()
        crossed[k - 1].wait_recv()
        far[k - 1].start()
    crossed[LINE - 1].wait_recv()
    far[LINE - 1].start()
    for k in range(LINE):
        crossing[k].wait_send()
        near[k].wait_send()
        far[k].wait_send()
        other = place.at(lines[k], place.x, 1 - place.core)
        other_far = place.at(lines[k], 1 - place.x, 1 - place.core)
        send(other, cs, k, cr, k, place.partner).wait_recv()
        send(other_far, cs, LINE + k, cr, LINE + k, place.partner).wait_recv()

    edge_own.wait_send()

    @pl.when(inner == 1)
    def _():
        out_own.wait_send()
        for relay in relays:
            relay.wait_send()


def gather_call(keys, values):
    rows = keys.shape[0]
    return pl.pallas_call(
        gather_kernel,
        in_specs=[pl.BlockSpec(memory_space=pltpu.VMEM)] * 2,
        out_specs=pl.BlockSpec(memory_space=pltpu.VMEM),
        out_shape=jax.ShapeDtypeStruct((SEQ, rows, 2 * HD), keys.dtype),
        scratch_shapes=[
            pltpu.SemaphoreType.DMA((5,)),
            pltpu.SemaphoreType.DMA((LINE,)),
            pltpu.SemaphoreType.DMA((LINE,)),
            pltpu.SemaphoreType.DMA((LINE,)),
            pltpu.SemaphoreType.DMA((2 * LINE,)),
            pltpu.SemaphoreType.DMA((2 * LINE,)),
        ],
        compiler_params=pltpu.CompilerParams(
            collective_id=0, has_side_effects=True, vmem_limit_bytes=32 * 1024 * 1024
        ),
        name="gather_blocks",
    )(keys, values)


def scatter_kernel(
    sums_ref, key_ref, value_ref, pair, cross_out, cross_in, line_out, line_in,
    ps, pr, xs, xr, zs, zr,
):
    place = Place()
    z, high, inner = place.z, place.high, place.inner
    wide = jnp.float32
    order = [3 * (1 - high), 2 - high, 1 - z + 4 * high, z]
    greet(place)

    def paired(side, k):
        x = 1 - place.x if side == 0 else place.x
        index = side * LINE + k
        source = sums_ref.at[place.at(order[k], x, 1 - place.core)]
        return remote(source, pair.at[index], ps.at[index], pr.at[index], place.partner)

    pairs = [[paired(side, k) for k in range(LINE)] for side in range(2)]
    crosses = [
        remote(cross_out.at[k], cross_in.at[k], xs.at[k], xr.at[k], place.across)
        for k in range(LINE)
    ]

    def hop(k, slot, device):
        return remote(line_out.at[k], line_in.at[slot], zs.at[k], zr.at[slot], device)

    for side in range(2):
        for k in range(LINE):
            pairs[side][k].start()
    for k in range(LINE):
        pairs[0][k].wait_recv()
        kept = sums_ref[place.at(order[k], 1 - place.x, place.core)]
        cross_out[k] = (kept.astype(wide) + pair[k].astype(wide)).astype(cross_out.dtype)
        crosses[k].start()

    def local(k):
        kept = sums_ref[place.at(order[k], place.x, place.core)].astype(wide)
        return kept + pair[LINE + k].astype(wide) + cross_in[k].astype(wide)

    def arrived(slot):
        hop(0, slot, place.onward).wait_recv()
        return line_in[slot].astype(wide)

    for k in range(LINE - 1):
        pairs[1][k].wait_recv()
        crosses[k].wait_recv()

        @pl.when(inner == 0)
        def _(k=k):
            line_out[k] = local(k).astype(line_out.dtype)
            hop(k, k, place.onward).start()

        @pl.when(inner == 1)
        def _(k=k):
            total = local(k) + arrived(k if k < 2 else 3)
            line_out[k] = total.astype(line_out.dtype)
            if k < 2:
                hop(k, 3 + k, place.onward).start()
            else:
                hop(k, 0, place.outward).start()

    pairs[1][LINE - 1].wait_recv()
    crosses[LINE - 1].wait_recv()

    def finish(total):
        key_ref[...] = total[:, :HD].astype(key_ref.dtype)
        value_ref[...] = total[:, HD:].astype(value_ref.dtype)

    @pl.when(inner == 0)
    def _():
        finish(local(LINE - 1) + arrived(0))

    @pl.when(inner == 1)
    def _():
        finish(local(LINE - 1) + arrived(2) + arrived(4))

    for k in range(LINE):
        pairs[0][k].wait_send()
        pairs[1][k].wait_send()
        crosses[k].wait_send()
    for k in range(LINE - 1):
        hop(k, k, place.onward).wait_send()


def scatter_call(sums):
    rows = sums.shape[1]
    half = jnp.bfloat16

    def slots(count):
        return pltpu.VMEM((count, rows, 2 * HD), half)

    return pl.pallas_call(
        scatter_kernel,
        in_specs=[pl.BlockSpec(memory_space=pltpu.VMEM)],
        out_specs=[pl.BlockSpec(memory_space=pltpu.VMEM)] * 2,
        out_shape=[jax.ShapeDtypeStruct((rows, HD), half)] * 2,
        scratch_shapes=[
            slots(2 * LINE),
            slots(LINE),
            slots(LINE),
            slots(LINE - 1),
            slots(5),
            pltpu.SemaphoreType.DMA((2 * LINE,)),
            pltpu.SemaphoreType.DMA((2 * LINE,)),
            pltpu.SemaphoreType.DMA((LINE,)),
            pltpu.SemaphoreType.DMA((LINE,)),
            pltpu.SemaphoreType.DMA((LINE - 1,)),
            pltpu.SemaphoreType.DMA((5,)),
        ],
        compiler_params=pltpu.CompilerParams(
            collective_id=1, has_side_effects=True, vmem_limit_bytes=40 * 1024 * 1024
        ),
        name="scatter_sums",
    )(sums)


def dense_body(queries, key_rows, value_rows, out_grads, segment_ids, random_blocks, global_blocks):
    qcount = queries.shape[0] // BLK
    position = lax.axis_index("seq")
    total_blocks = segment_ids.shape[0] // BLK
    kv = gather_call(key_rows, value_rows).reshape(total_blocks, BLK, 2 * HD)
    boundary = jnp.sum((segment_ids == segment_ids[0]).astype(jnp.int32))
    meta = jnp.stack([boundary, (position * qcount).astype(jnp.int32)])
    attended, query_grads, sums = attention_call(
        meta, random_blocks.reshape(-1), global_blocks, queries, out_grads, kv
    )
    key_grads, value_grads = scatter_call(sums.reshape(SEQ, -1, 2 * HD))
    return (attended, query_grads, key_grads, value_grads)


def plan(*arrays):
    tokens = arrays[4].shape[0]
    fits = tokens * 2 * HD * 4 <= DENSE_BYTES
    chosen = dense_body if fits and lax.axis_size("seq") == SEQ else body
    return chosen(*arrays)


def solution(mesh):
    placed = (
        P(("shard", "seq"), None),
        P(("shard", "seq"), None),
        P(("shard", "seq"), None),
        P(("shard", "seq"), None),
        P("shard"),
        P(("shard", "seq"), None, None),
        P("shard"),
    )
    return jax.shard_map(
        plan,
        mesh=mesh,
        in_specs=placed,
        out_specs=(
            P(("shard", "seq"), None),
            P(("shard", "seq"), None),
            P(("shard", "seq"), None),
            P(("shard", "seq"), None),
        ),
        check_vma=False,
    )
```

```python
import math

import jax
import jax.numpy as jnp
from jax import lax
from jax.experimental import pallas as pl
from jax.experimental.pallas import tpu as pltpu
from jax.sharding import PartitionSpec as P

HD = 128
HQ = 8
BLK = 128
RAND = 3
G = 2


masked_value = -1e30


def with_halo(array, sides, width):
    for axis, dim in sides:
        size, length = (lax.axis_size(axis), array.shape[dim])
        up = [(i, (i + 1) % size) for i in range(size - 1)]
        down = [(j, i) for i, j in up]
        last = lax.slice_in_dim(array, length - width, length, axis=dim)
        first = lax.slice_in_dim(array, 0, width, axis=dim)
        before = lax.ppermute(last, axis, up)
        after = lax.ppermute(first, axis, down)
        array = jnp.concatenate([before, array, after], axis=dim)
    return array


def spread(block, axis, owner):
    block = jnp.where(lax.axis_index(axis) == owner, block, jnp.zeros_like(block))
    return lax.psum(block, axis)


def from_behind(block, axis, distance):
    devices = range(lax.axis_size(axis))
    route = [(i - distance, i) for i in devices if i - distance in devices]
    return lax.ppermute(block, axis, route)


def routing(block_ids, per_device):
    owners = block_ids // per_device
    ordering = jnp.arange(block_ids.shape[0])
    earlier = (owners[:, None] == owners[None, :]) & (ordering[None, :] < ordering[:, None])
    return (owners, jnp.sum(earlier.astype(jnp.int32), axis=1))


def block_pass(
    query_block,
    grad_block,
    shared,
    shared_live,
    query_segs,
    shared_segs,
    random_kv,
    random_segs,
    scaling,
):
    wide = jnp.float32
    shared_mask = (query_segs[:, None, None] == shared_segs[None]) & shared_live[None, :, None]
    random_mask = query_segs[None, :, None, None] == random_segs[:, None]
    shared_scores = (
        jnp.einsum("thd,jkd->htjk", query_block, shared[:, :, :HD], preferred_element_type=wide)
        * scaling
    )
    shared_scores = jnp.where(shared_mask[None], shared_scores, masked_value)
    random_scores = (
        jnp.einsum(
            "thd,hrkd->htrk", query_block, random_kv[:, :, :, :HD], preferred_element_type=wide
        )
        * scaling
    )
    random_scores = jnp.where(random_mask, random_scores, masked_value)
    top_score = jnp.maximum(
        jnp.max(shared_scores, axis=(2, 3)), jnp.max(random_scores, axis=(2, 3))
    )
    totals = jnp.sum(jnp.exp(shared_scores - top_score[:, :, None, None]), axis=(2, 3))
    totals = totals + jnp.sum(jnp.exp(random_scores - top_score[:, :, None, None]), axis=(2, 3))
    log_totals = top_score + jnp.log(totals)
    shared_probs = jnp.exp(shared_scores - log_totals[:, :, None, None])
    random_probs = jnp.exp(random_scores - log_totals[:, :, None, None])
    shared_half = shared_probs.astype(jnp.bfloat16)
    random_half = random_probs.astype(jnp.bfloat16)
    attended = jnp.einsum(
        "htjk,jkd->thd", shared_half, shared[:, :, HD:], preferred_element_type=wide
    )
    attended = attended + jnp.einsum(
        "htrk,hrkd->thd", random_half, random_kv[:, :, :, HD:], preferred_element_type=wide
    )
    attended = attended.astype(jnp.bfloat16)
    row_dots = jnp.einsum("thd,thd->ht", grad_block, attended, preferred_element_type=wide)
    shared_dprobs = jnp.einsum(
        "thd,jkd->htjk", grad_block, shared[:, :, HD:], preferred_element_type=wide
    )
    random_dprobs = jnp.einsum(
        "thd,hrkd->htrk", grad_block, random_kv[:, :, :, HD:], preferred_element_type=wide
    )
    shared_dscores = (shared_probs * (shared_dprobs - row_dots[:, :, None, None])).astype(
        jnp.bfloat16
    )
    random_dscores = (random_probs * (random_dprobs - row_dots[:, :, None, None])).astype(
        jnp.bfloat16
    )
    query_grads = jnp.einsum(
        "htjk,jkd->thd", shared_dscores, shared[:, :, :HD], preferred_element_type=wide
    )
    query_grads = query_grads + jnp.einsum(
        "htrk,hrkd->thd", random_dscores, random_kv[:, :, :, :HD], preferred_element_type=wide
    )
    query_grads = (query_grads * scaling).astype(jnp.bfloat16)
    shared_kgrad = (
        jnp.einsum("htjk,thd->jkd", shared_dscores, query_block, preferred_element_type=wide)
        * scaling
    )
    shared_vgrad = jnp.einsum("htjk,thd->jkd", shared_half, grad_block, preferred_element_type=wide)
    shared_grads = jnp.where(
        shared_live[:, None, None], jnp.concatenate([shared_kgrad, shared_vgrad], axis=2), 0.0
    )
    random_kgrad = (
        jnp.einsum("htrk,thd->hrkd", random_dscores, query_block, preferred_element_type=wide)
        * scaling
    )
    random_vgrad = jnp.einsum(
        "htrk,thd->hrkd", random_half, grad_block, preferred_element_type=wide
    )
    random_grads = jnp.concatenate([random_kgrad, random_vgrad], axis=3)
    return (attended, query_grads, shared_grads, random_grads, log_totals, row_dots)


def body(queries, key_rows, value_rows, out_grads, segment_ids, random_blocks, global_blocks):
    scaling = 1.0 / math.sqrt(HD)
    row_count = queries.shape[0]
    qcount = row_count // BLK
    devices = lax.axis_size("seq")
    position = lax.axis_index("seq")
    total_blocks = segment_ids.shape[0] // BLK
    seg_blocks = segment_ids.reshape(total_blocks, BLK)
    joined = jnp.concatenate([key_rows, value_rows], axis=1)
    local_blocks = joined.reshape(qcount, BLK, 2 * HD)
    padded = with_halo(joined, (("seq", 0),), BLK)
    owned = global_blocks // qcount == position
    pieces = []
    for global_slot in range(G):
        picked = lax.dynamic_index_in_dim(
            local_blocks, global_blocks[global_slot] % qcount, 0, keepdims=False
        )
        pieces.append(spread(picked, "seq", global_blocks[global_slot] // qcount))
    global_kv = jnp.stack(pieces)
    chosen_ids = random_blocks.reshape(-1)
    pick_count = chosen_ids.shape[0]
    capacity = -(-pick_count // devices)
    owners, slots = routing(chosen_ids, qcount)
    outgoing_ids = (
        jnp.full((devices, capacity), -1, jnp.int32).at[owners, slots].set(chosen_ids % qcount)
    )
    wanted = lax.all_to_all(outgoing_ids, "seq", split_axis=0, concat_axis=0, tiled=True)
    wanted_clip = jnp.clip(wanted, 0, qcount - 1)
    served = local_blocks[wanted_clip]
    answer = lax.all_to_all(served, "seq", split_axis=0, concat_axis=0, tiled=True)
    random_kv = answer[owners, slots].reshape(qcount, HQ, RAND, BLK, 2 * HD)
    query_blocks = queries.reshape(qcount, BLK, HQ, HD)
    grad_blocks = out_grads.reshape(qcount, BLK, HQ, HD)

    def attend(bundle):
        block_index, query_block, grad_block, block_kv, block_ids = bundle
        global_index = position * qcount + block_index
        window = lax.dynamic_slice_in_dim(padded, block_index * BLK, 3 * BLK, 0).reshape(
            3, BLK, 2 * HD
        )
        window_ids = global_index + jnp.arange(-1, 2, dtype=jnp.int32)
        window_live = (window_ids >= 0) & (window_ids < total_blocks)
        shared_ids = jnp.concatenate([jnp.clip(window_ids, 0, total_blocks - 1), global_blocks])
        shared_live = jnp.concatenate([window_live, jnp.ones((G,), bool)])
        shared = jnp.concatenate([window, global_kv], axis=0)
        return block_pass(
            query_block,
            grad_block,
            shared,
            shared_live,
            seg_blocks[global_index],
            seg_blocks[shared_ids],
            block_kv,
            seg_blocks[block_ids],
            scaling,
        )

    attended, query_grads, shared_grads, random_grads, log_totals, row_dots = lax.map(
        attend,
        (jnp.arange(qcount, dtype=jnp.int32), query_blocks, grad_blocks, random_kv, random_blocks),
    )
    window_sum = jnp.zeros((qcount + 2, BLK, 2 * HD), jnp.float32)
    for offset in range(3):
        window_sum = window_sum.at[offset : offset + qcount].add(shared_grads[:, offset])
    from_right = from_behind(window_sum[0].astype(jnp.bfloat16), "seq", -1).astype(jnp.float32)
    from_left = from_behind(window_sum[qcount + 1].astype(jnp.bfloat16), "seq", 1).astype(
        jnp.float32
    )
    own_grads = window_sum[1 : qcount + 1]
    own_grads = own_grads.at[qcount - 1].add(from_right).at[0].add(from_left)
    global_sum = lax.psum(jnp.sum(shared_grads[:, 3:], axis=0), "seq")
    global_hits = (
        (global_blocks[:, None] % qcount == jnp.arange(qcount)[None, :]) & owned[:, None]
    ).astype(jnp.float32)
    own_grads = own_grads + jnp.einsum(
        "gq,gkd->qkd", global_hits, global_sum, precision=lax.Precision.HIGHEST
    )
    outgoing = (
        jnp.zeros((devices, capacity, BLK, 2 * HD), jnp.float32)
        .at[owners, slots]
        .set(random_grads.reshape(pick_count, BLK, 2 * HD))
    )
    returned = lax.all_to_all(outgoing, "seq", split_axis=0, concat_axis=0, tiled=True)
    request_hits = (wanted[:, :, None] == jnp.arange(qcount)[None, None, :]).astype(jnp.float32)
    own_grads = own_grads + jnp.einsum(
        "ncq,nckd->qkd", request_hits, returned, precision=lax.Precision.HIGHEST
    )
    own_flat = own_grads.reshape(row_count, 2 * HD)
    return (
        attended.reshape(row_count, HQ * HD),
        query_grads.reshape(row_count, HQ * HD),
        own_flat[:, :HD].astype(jnp.bfloat16),
        own_flat[:, HD:].astype(jnp.bfloat16),
    )


SUM_TYPE = jnp.bfloat16
LOG2E = 1.4426950408889634
DENSE_BYTES = 16 * 1024 * 1024


def attention_kernel(
    random_ref,
    global_ref,
    segment_ref,
    query_ref,
    grad_ref,
    kv_ref,
    kvt_ref,
    attended_ref,
    query_grad_ref,
    sums_ref,
    acc_ref,
):
    wide = jnp.float32
    total_blocks = kv_ref.shape[0]
    qcount = query_ref.shape[0] // BLK
    scaling = 1.0 / math.sqrt(HD)
    first = lax.axis_index("seq") * qcount
    boundary = jnp.sum((segment_ref[...] == segment_ref[0:1, 0:1]).astype(jnp.int32))

    @pl.loop(0, total_blocks)
    def _(index):
        acc_ref[index] = jnp.zeros((BLK, 2 * HD), wide)

    @pl.loop(0, qcount)
    def _(block):
        attend_block(
            block,
            first + block,
            boundary,
            random_ref,
            global_ref,
            query_ref,
            grad_ref,
            kv_ref,
            kvt_ref,
            attended_ref,
            query_grad_ref,
            acc_ref,
        )

    @pl.loop(0, total_blocks)
    def _(index):
        sums_ref[index, :, :HD] = (acc_ref[index, :, :HD] * scaling).astype(sums_ref.dtype)
        sums_ref[index, :, HD:] = acc_ref[index, :, HD:].astype(sums_ref.dtype)


def attend_block(
    block,
    mine,
    boundary,
    random_ref,
    global_ref,
    query_ref,
    grad_ref,
    kv_ref,
    kvt_ref,
    attended_ref,
    query_grad_ref,
    acc_ref,
):
    wide = jnp.float32
    half = jnp.bfloat16
    total_blocks = kv_ref.shape[0]
    heads = HQ
    scaling = 1.0 / math.sqrt(HD)
    rows = pl.ds(pl.multiple_of(block * BLK, BLK), BLK)
    shared_ids = [
        jnp.maximum(mine - 1, 0),
        mine,
        jnp.minimum(mine + 1, total_blocks - 1),
        global_ref[0],
        global_ref[1],
    ]
    dead = [
        jnp.where(mine == 0, masked_value, 0.0).astype(wide),
        None,
        jnp.where(mine == total_blocks - 1, masked_value, 0.0).astype(wide),
        None,
        None,
    ]
    random_ids = [[random_ref[pick, block, head] for head in range(heads)] for pick in range(RAND)]

    queries = [query_ref[rows, head * HD : (head + 1) * HD] for head in range(heads)]
    grads = [grad_ref[rows, head * HD : (head + 1) * HD] for head in range(heads)]
    query_stack = jnp.concatenate(queries, axis=0)
    grad_stack = jnp.concatenate(grads, axis=0)

    def against(rows, columns):
        return lax.dot_general(rows, columns, (((1,), (1,)), ((), ())), preferred_element_type=wide)

    def product(rows, columns):
        return jnp.dot(rows, columns, preferred_element_type=wide)

    def entries(start, stack, parts):
        tiles = [against(kv_ref[i, :, start : start + HD], stack) for i in shared_ids]
        for names in random_ids:
            tiles.append(
                jnp.concatenate(
                    [
                        against(kv_ref[i, :, start : start + HD], part)
                        for i, part in zip(names, parts)
                    ],
                    axis=1,
                )
            )
        return tiles

    key_row = lax.broadcasted_iota(jnp.int32, (BLK, HD), 0)
    query_low = lax.broadcasted_iota(jnp.int32, (BLK, HD), 1) < boundary - mine * BLK

    def allowed(name):
        return (key_row < boundary - name * BLK) == query_low

    scores = entries(0, query_stack, queries)
    factor = scaling * LOG2E
    masked = []
    for slot, tile in enumerate(scores):
        pieces = []
        for head in range(heads):
            piece = tile[:, head * BLK : (head + 1) * BLK] * factor
            name = shared_ids[slot] if slot < 5 else random_ids[slot - 5][head]
            piece = jnp.where(allowed(name), piece, masked_value)
            if slot < 5 and dead[slot] is not None:
                piece = piece + dead[slot]
            pieces.append(piece)
        masked.append(jnp.concatenate(pieces, axis=1))
    top = masked[0]
    for tile in masked[1:]:
        top = jnp.maximum(top, tile)
    top = jnp.max(top, axis=0, keepdims=True)
    powers = [jnp.exp2(tile - top) for tile in masked]
    total = powers[0]
    for tile in powers[1:]:
        total = total + tile
    inverse = 1.0 / jnp.sum(total, axis=0, keepdims=True)
    probs = [tile * inverse for tile in powers]
    probs_half = [tile.astype(half) for tile in probs]

    def gathered(start, tiles):
        shared = product(
            jnp.concatenate([kvt_ref[i, start : start + HD, :] for i in shared_ids], axis=1),
            jnp.concatenate(tiles[:5], axis=0),
        )
        pieces = []
        for head in range(heads):
            names = [random_ids[pick][head] for pick in range(RAND)]
            pieces.append(
                product(
                    jnp.concatenate([kvt_ref[i, start : start + HD, :] for i in names], axis=1),
                    jnp.concatenate(
                        [tile[:, head * BLK : (head + 1) * BLK] for tile in tiles[5:]], axis=0
                    ),
                )
            )
        return shared + jnp.concatenate(pieces, axis=1)

    attended = gathered(HD, probs_half).astype(half).astype(wide)
    grads_turned = jnp.concatenate([part.astype(wide).T for part in grads], axis=1)
    row_dots = jnp.sum(attended * grads_turned, axis=0, keepdims=True)
    for head in range(heads):
        span = slice(head * BLK, (head + 1) * BLK)
        attended_ref[rows, span] = attended[:, span].T.astype(half)
    dprobs = entries(HD, grad_stack, grads)
    dscores = [(p * (d - row_dots)).astype(half) for p, d in zip(probs, dprobs)]
    query_grads = gathered(0, dscores) * scaling
    for head in range(heads):
        span = slice(head * BLK, (head + 1) * BLK)
        query_grad_ref[rows, span] = query_grads[:, span].T.astype(half)
    for slot, name in enumerate(shared_ids):
        acc_ref[name, :, :HD] += product(dscores[slot], query_stack)
        acc_ref[name, :, HD:] += product(probs_half[slot], grad_stack)
    for pick in range(RAND):
        for head in range(heads):
            name = random_ids[pick][head]
            span = slice(head * BLK, (head + 1) * BLK)
            acc_ref[name, :, :HD] += product(dscores[5 + pick][:, span], queries[head])
            acc_ref[name, :, HD:] += product(probs_half[5 + pick][:, span], grads[head])


def attention_call(random_ids, global_ids, segments, queries, out_grads, kv, kvt):
    vmem = pl.BlockSpec(memory_space=pltpu.VMEM)
    smem = pl.BlockSpec(memory_space=pltpu.SMEM)
    return pl.pallas_call(
        attention_kernel,
        in_specs=[smem, smem] + [vmem] * 5,
        out_specs=[vmem] * 3,
        scratch_shapes=[pltpu.VMEM(kv.shape, jnp.float32)],
        out_shape=[
            jax.ShapeDtypeStruct(queries.shape, jnp.bfloat16),
            jax.ShapeDtypeStruct(queries.shape, jnp.bfloat16),
            jax.ShapeDtypeStruct(kv.shape, SUM_TYPE),
        ],
        compiler_params=pltpu.CompilerParams(vmem_limit_bytes=ATTEND_MIB * 1024 * 1024),
        name="block_attention",
    )(random_ids, global_ids, segments, queries, out_grads, kv, kvt)


ATTEND_MIB = 32
LINE = 4
SEQ = 16


class Place:
    def __init__(self):
        me = lax.axis_index("seq")
        self.me = me
        self.core = lax.rem(me, 2)
        self.x = lax.rem(me // 2, 2)
        self.z = me // 4
        self.high = self.z // 2
        self.step = 1 - 2 * self.high
        self.inner = jnp.where((self.z == 1) | (self.z == 2), 1, 0)
        self.partner = self.at(self.z, self.x, 1 - self.core)
        self.across = self.at(self.z, 1 - self.x, self.core)
        self.onward = self.at(self.z + self.step, self.x, self.core)
        self.outward = self.at(self.z - self.step, self.x, self.core)

    def at(self, z, x, core):
        return z * 4 + x * 2 + core


def greet(place):
    barrier = pltpu.get_barrier_semaphore()
    for other in (place.partner, place.across, place.onward):
        pl.semaphore_signal(
            barrier, inc=1, device_id={"seq": other}, device_id_type=pl.DeviceIdType.MESH
        )

    @pl.when(place.inner == 1)
    def _():
        pl.semaphore_signal(
            barrier, inc=1, device_id={"seq": place.outward}, device_id_type=pl.DeviceIdType.MESH
        )

    pl.semaphore_wait(barrier, 3 + place.inner)


def remote(source, target, send, receive, device):
    return pltpu.make_async_remote_copy(
        src_ref=source,
        dst_ref=target,
        send_sem=send,
        recv_sem=receive,
        device_id={"seq": device},
        device_id_type=pl.DeviceIdType.MESH,
    )


def gather_kernel(key_ref, value_ref, out_ref, turned_ref, zs, zr, xs, xr, cs, cr):
    place = Place()
    z, step, inner = place.z, place.step, place.inner
    lines = [z, z + step - 2 * step * inner, z + step * (2 - inner), z + step * (3 - inner)]
    mine = [place.at(line, place.x, place.core) for line in lines]
    theirs = [place.at(line, 1 - place.x, place.core) for line in lines]
    out_ref[place.me, :, :HD] = key_ref[...]
    out_ref[place.me, :, HD:] = value_ref[...]
    greet(place)

    def send(slot, sends, index, receives, to, device):
        return remote(
            out_ref.at[slot], out_ref.at[slot], sends.at[index], receives.at[to], device
        )

    along = [send(mine[0], zs, 0, zr, 2, place.onward)]
    edge_own = send(mine[0], zs, 0, zr, 1, place.onward)
    out_own = send(mine[0], zs, 1, zr, 1, place.outward)
    relays = [
        send(mine[1], zs, 2, zr, 3, place.onward),
        send(mine[2], zs, 3, zr, 2, place.outward),
        send(mine[3], zs, 4, zr, 3, place.outward),
    ]
    arrivals = [
        send(mine[index], zs, 0, zr, index, place.onward) for index in range(1, LINE)
    ]
    crossing = [send(mine[k], xs, k, xr, k, place.across) for k in range(LINE)]
    crossed = [send(theirs[k], xs, k, xr, k, place.across) for k in range(LINE)]
    near = [send(mine[k], cs, k, cr, k, place.partner) for k in range(LINE)]
    far = [send(theirs[k], cs, LINE + k, cr, LINE + k, place.partner) for k in range(LINE)]

    @pl.when(inner == 0)
    def _():
        edge_own.start()

    @pl.when(inner == 1)
    def _():
        along[0].start()
        out_own.start()

    crossing[0].start()
    near[0].start()
    pieces = key_ref.shape[0] // BLK

    def turn(slot):
        for piece in range(pieces):
            rows = slice(piece * BLK, (piece + 1) * BLK)
            turned_ref[slot * pieces + piece] = out_ref[slot, rows, :].T

    def turn_partner(k):
        other = place.at(lines[k], place.x, 1 - place.core)
        other_far = place.at(lines[k], 1 - place.x, 1 - place.core)
        send(other, cs, k, cr, k, place.partner).wait_recv()
        turn(other)
        send(other_far, cs, LINE + k, cr, LINE + k, place.partner).wait_recv()
        turn(other_far)

    for k in range(1, LINE):
        arrivals[k - 1].wait_recv()

        @pl.when(inner == 1)
        def _(k=k):
            relays[k - 1].start()

        crossing[k].start()
        near[k].start()
        turn(mine[k - 1])
        crossed[k - 1].wait_recv()
        far[k - 1].start()
        turn(theirs[k - 1])
        if k > 1:
            turn_partner(k - 2)
    turn(mine[LINE - 1])
    turn_partner(LINE - 2)
    crossed[LINE - 1].wait_recv()
    far[LINE - 1].start()
    turn(theirs[LINE - 1])
    turn_partner(LINE - 1)
    for k in range(LINE):
        crossing[k].wait_send()
        near[k].wait_send()
        far[k].wait_send()

    edge_own.wait_send()

    @pl.when(inner == 1)
    def _():
        out_own.wait_send()
        for relay in relays:
            relay.wait_send()


def gather_call(keys, values):
    rows = keys.shape[0]
    return pl.pallas_call(
        gather_kernel,
        in_specs=[pl.BlockSpec(memory_space=pltpu.VMEM)] * 2,
        out_specs=[pl.BlockSpec(memory_space=pltpu.VMEM)] * 2,
        out_shape=[
            jax.ShapeDtypeStruct((SEQ, rows, 2 * HD), keys.dtype),
            jax.ShapeDtypeStruct((SEQ * rows // BLK, 2 * HD, BLK), keys.dtype),
        ],
        scratch_shapes=[
            pltpu.SemaphoreType.DMA((5,)),
            pltpu.SemaphoreType.DMA((LINE,)),
            pltpu.SemaphoreType.DMA((LINE,)),
            pltpu.SemaphoreType.DMA((LINE,)),
            pltpu.SemaphoreType.DMA((2 * LINE,)),
            pltpu.SemaphoreType.DMA((2 * LINE,)),
        ],
        compiler_params=pltpu.CompilerParams(
            collective_id=0, has_side_effects=True, vmem_limit_bytes=32 * 1024 * 1024
        ),
        name="gather_blocks",
    )(keys, values)


def scatter_kernel(
    sums_ref, key_ref, value_ref, pair, cross_out, cross_in, line_out, line_in,
    ps, pr, xs, xr, zs, zr,
):
    place = Place()
    z, high, inner = place.z, place.high, place.inner
    wide = jnp.float32
    order = [3 * (1 - high), 2 - high, 1 - z + 4 * high, z]
    greet(place)

    def paired(side, k):
        x = 1 - place.x if side == 0 else place.x
        index = side * LINE + k
        source = sums_ref.at[place.at(order[k], x, 1 - place.core)]
        return remote(source, pair.at[index], ps.at[index], pr.at[index], place.partner)

    pairs = [[paired(side, k) for k in range(LINE)] for side in range(2)]
    crosses = [
        remote(cross_out.at[k], cross_in.at[k], xs.at[k], xr.at[k], place.across)
        for k in range(LINE)
    ]

    def hop(k, slot, device):
        return remote(line_out.at[k], line_in.at[slot], zs.at[k], zr.at[slot], device)

    for side in range(2):
        for k in range(LINE):
            pairs[side][k].start()
    for k in range(LINE):
        pairs[0][k].wait_recv()
        kept = sums_ref[place.at(order[k], 1 - place.x, place.core)]
        cross_out[k] = (kept.astype(wide) + pair[k].astype(wide)).astype(cross_out.dtype)
        crosses[k].start()

    def local(k):
        kept = sums_ref[place.at(order[k], place.x, place.core)].astype(wide)
        return kept + pair[LINE + k].astype(wide) + cross_in[k].astype(wide)

    def arrived(slot):
        hop(0, slot, place.onward).wait_recv()
        return line_in[slot].astype(wide)

    for k in range(LINE - 1):
        pairs[1][k].wait_recv()
        crosses[k].wait_recv()

        @pl.when(inner == 0)
        def _(k=k):
            line_out[k] = local(k).astype(line_out.dtype)
            hop(k, k, place.onward).start()

        @pl.when(inner == 1)
        def _(k=k):
            total = local(k) + arrived(k if k < 2 else 3)
            line_out[k] = total.astype(line_out.dtype)
            if k < 2:
                hop(k, 3 + k, place.onward).start()
            else:
                hop(k, 0, place.outward).start()

    pairs[1][LINE - 1].wait_recv()
    crosses[LINE - 1].wait_recv()

    def finish(total):
        key_ref[...] = total[:, :HD].astype(key_ref.dtype)
        value_ref[...] = total[:, HD:].astype(value_ref.dtype)

    @pl.when(inner == 0)
    def _():
        finish(local(LINE - 1) + arrived(0))

    @pl.when(inner == 1)
    def _():
        finish(local(LINE - 1) + arrived(2) + arrived(4))

    for k in range(LINE):
        pairs[0][k].wait_send()
        pairs[1][k].wait_send()
        crosses[k].wait_send()
    for k in range(LINE - 1):
        hop(k, k, place.onward).wait_send()


def scatter_call(sums):
    rows = sums.shape[1]
    half = jnp.bfloat16

    def slots(count):
        return pltpu.VMEM((count, rows, 2 * HD), half)

    return pl.pallas_call(
        scatter_kernel,
        in_specs=[pl.BlockSpec(memory_space=pltpu.VMEM)],
        out_specs=[pl.BlockSpec(memory_space=pltpu.VMEM)] * 2,
        out_shape=[jax.ShapeDtypeStruct((rows, HD), half)] * 2,
        scratch_shapes=[
            slots(2 * LINE),
            slots(LINE),
            slots(LINE),
            slots(LINE - 1),
            slots(5),
            pltpu.SemaphoreType.DMA((2 * LINE,)),
            pltpu.SemaphoreType.DMA((2 * LINE,)),
            pltpu.SemaphoreType.DMA((LINE,)),
            pltpu.SemaphoreType.DMA((LINE,)),
            pltpu.SemaphoreType.DMA((LINE - 1,)),
            pltpu.SemaphoreType.DMA((5,)),
        ],
        compiler_params=pltpu.CompilerParams(
            collective_id=1, has_side_effects=True, vmem_limit_bytes=40 * 1024 * 1024
        ),
        name="scatter_sums",
    )(sums)


def dense_body(queries, key_rows, value_rows, out_grads, segment_ids, random_blocks, global_blocks):
    total_blocks = segment_ids.shape[0] // BLK
    kv, kvt = gather_call(key_rows, value_rows)
    kv = kv.reshape(total_blocks, BLK, 2 * HD)
    attended, query_grads, sums = attention_call(
        random_blocks.transpose(2, 0, 1), global_blocks, segment_ids.reshape(total_blocks, BLK), queries,
        out_grads, kv, kvt,
    )
    key_grads, value_grads = scatter_call(sums.reshape(SEQ, -1, 2 * HD))
    return (attended, query_grads, key_grads, value_grads)


def plan(*arrays):
    tokens = arrays[4].shape[0]
    fits = tokens * 2 * HD * 4 <= DENSE_BYTES
    chosen = dense_body if fits and lax.axis_size("seq") == SEQ else body
    return chosen(*arrays)


def solution(mesh):
    placed = (
        P(("shard", "seq"), None),
        P(("shard", "seq"), None),
        P(("shard", "seq"), None),
        P(("shard", "seq"), None),
        P("shard"),
        P(("shard", "seq"), None, None),
        P("shard"),
    )
    return jax.shard_map(
        plan,
        mesh=mesh,
        in_specs=placed,
        out_specs=(
            P(("shard", "seq"), None),
            P(("shard", "seq"), None),
            P(("shard", "seq"), None),
            P(("shard", "seq"), None),
        ),
        check_vma=False,
    )
```

```python
import math

import jax
import jax.numpy as jnp
from jax import lax
from jax.experimental import pallas as pl
from jax.experimental.pallas import tpu as pltpu
from jax.sharding import PartitionSpec as P

HD = 128
HQ = 8
BLK = 128
RAND = 3
G = 2


masked_value = -1e30


def with_halo(array, sides, width):
    for axis, dim in sides:
        size, length = (lax.axis_size(axis), array.shape[dim])
        up = [(i, (i + 1) % size) for i in range(size - 1)]
        down = [(j, i) for i, j in up]
        last = lax.slice_in_dim(array, length - width, length, axis=dim)
        first = lax.slice_in_dim(array, 0, width, axis=dim)
        before = lax.ppermute(last, axis, up)
        after = lax.ppermute(first, axis, down)
        array = jnp.concatenate([before, array, after], axis=dim)
    return array


def spread(block, axis, owner):
    block = jnp.where(lax.axis_index(axis) == owner, block, jnp.zeros_like(block))
    return lax.psum(block, axis)


def from_behind(block, axis, distance):
    devices = range(lax.axis_size(axis))
    route = [(i - distance, i) for i in devices if i - distance in devices]
    return lax.ppermute(block, axis, route)


def routing(block_ids, per_device):
    owners = block_ids // per_device
    ordering = jnp.arange(block_ids.shape[0])
    earlier = (owners[:, None] == owners[None, :]) & (ordering[None, :] < ordering[:, None])
    return (owners, jnp.sum(earlier.astype(jnp.int32), axis=1))


def block_pass(
    query_block,
    grad_block,
    shared,
    shared_live,
    query_segs,
    shared_segs,
    random_kv,
    random_segs,
    scaling,
):
    wide = jnp.float32
    shared_mask = (query_segs[:, None, None] == shared_segs[None]) & shared_live[None, :, None]
    random_mask = query_segs[None, :, None, None] == random_segs[:, None]
    shared_scores = (
        jnp.einsum("thd,jkd->htjk", query_block, shared[:, :, :HD], preferred_element_type=wide)
        * scaling
    )
    shared_scores = jnp.where(shared_mask[None], shared_scores, masked_value)
    random_scores = (
        jnp.einsum(
            "thd,hrkd->htrk", query_block, random_kv[:, :, :, :HD], preferred_element_type=wide
        )
        * scaling
    )
    random_scores = jnp.where(random_mask, random_scores, masked_value)
    top_score = jnp.maximum(
        jnp.max(shared_scores, axis=(2, 3)), jnp.max(random_scores, axis=(2, 3))
    )
    totals = jnp.sum(jnp.exp(shared_scores - top_score[:, :, None, None]), axis=(2, 3))
    totals = totals + jnp.sum(jnp.exp(random_scores - top_score[:, :, None, None]), axis=(2, 3))
    log_totals = top_score + jnp.log(totals)
    shared_probs = jnp.exp(shared_scores - log_totals[:, :, None, None])
    random_probs = jnp.exp(random_scores - log_totals[:, :, None, None])
    shared_half = shared_probs.astype(jnp.bfloat16)
    random_half = random_probs.astype(jnp.bfloat16)
    attended = jnp.einsum(
        "htjk,jkd->thd", shared_half, shared[:, :, HD:], preferred_element_type=wide
    )
    attended = attended + jnp.einsum(
        "htrk,hrkd->thd", random_half, random_kv[:, :, :, HD:], preferred_element_type=wide
    )
    attended = attended.astype(jnp.bfloat16)
    row_dots = jnp.einsum("thd,thd->ht", grad_block, attended, preferred_element_type=wide)
    shared_dprobs = jnp.einsum(
        "thd,jkd->htjk", grad_block, shared[:, :, HD:], preferred_element_type=wide
    )
    random_dprobs = jnp.einsum(
        "thd,hrkd->htrk", grad_block, random_kv[:, :, :, HD:], preferred_element_type=wide
    )
    shared_dscores = (shared_probs * (shared_dprobs - row_dots[:, :, None, None])).astype(
        jnp.bfloat16
    )
    random_dscores = (random_probs * (random_dprobs - row_dots[:, :, None, None])).astype(
        jnp.bfloat16
    )
    query_grads = jnp.einsum(
        "htjk,jkd->thd", shared_dscores, shared[:, :, :HD], preferred_element_type=wide
    )
    query_grads = query_grads + jnp.einsum(
        "htrk,hrkd->thd", random_dscores, random_kv[:, :, :, :HD], preferred_element_type=wide
    )
    query_grads = (query_grads * scaling).astype(jnp.bfloat16)
    shared_kgrad = (
        jnp.einsum("htjk,thd->jkd", shared_dscores, query_block, preferred_element_type=wide)
        * scaling
    )
    shared_vgrad = jnp.einsum("htjk,thd->jkd", shared_half, grad_block, preferred_element_type=wide)
    shared_grads = jnp.where(
        shared_live[:, None, None], jnp.concatenate([shared_kgrad, shared_vgrad], axis=2), 0.0
    )
    random_kgrad = (
        jnp.einsum("htrk,thd->hrkd", random_dscores, query_block, preferred_element_type=wide)
        * scaling
    )
    random_vgrad = jnp.einsum(
        "htrk,thd->hrkd", random_half, grad_block, preferred_element_type=wide
    )
    random_grads = jnp.concatenate([random_kgrad, random_vgrad], axis=3)
    return (attended, query_grads, shared_grads, random_grads, log_totals, row_dots)


def body(queries, key_rows, value_rows, out_grads, segment_ids, random_blocks, global_blocks):
    scaling = 1.0 / math.sqrt(HD)
    row_count = queries.shape[0]
    qcount = row_count // BLK
    devices = lax.axis_size("seq")
    position = lax.axis_index("seq")
    total_blocks = segment_ids.shape[0] // BLK
    seg_blocks = segment_ids.reshape(total_blocks, BLK)
    joined = jnp.concatenate([key_rows, value_rows], axis=1)
    local_blocks = joined.reshape(qcount, BLK, 2 * HD)
    padded = with_halo(joined, (("seq", 0),), BLK)
    owned = global_blocks // qcount == position
    pieces = []
    for global_slot in range(G):
        picked = lax.dynamic_index_in_dim(
            local_blocks, global_blocks[global_slot] % qcount, 0, keepdims=False
        )
        pieces.append(spread(picked, "seq", global_blocks[global_slot] // qcount))
    global_kv = jnp.stack(pieces)
    chosen_ids = random_blocks.reshape(-1)
    pick_count = chosen_ids.shape[0]
    capacity = -(-pick_count // devices)
    owners, slots = routing(chosen_ids, qcount)
    outgoing_ids = (
        jnp.full((devices, capacity), -1, jnp.int32).at[owners, slots].set(chosen_ids % qcount)
    )
    wanted = lax.all_to_all(outgoing_ids, "seq", split_axis=0, concat_axis=0, tiled=True)
    wanted_clip = jnp.clip(wanted, 0, qcount - 1)
    served = local_blocks[wanted_clip]
    answer = lax.all_to_all(served, "seq", split_axis=0, concat_axis=0, tiled=True)
    random_kv = answer[owners, slots].reshape(qcount, HQ, RAND, BLK, 2 * HD)
    query_blocks = queries.reshape(qcount, BLK, HQ, HD)
    grad_blocks = out_grads.reshape(qcount, BLK, HQ, HD)

    def attend(bundle):
        block_index, query_block, grad_block, block_kv, block_ids = bundle
        global_index = position * qcount + block_index
        window = lax.dynamic_slice_in_dim(padded, block_index * BLK, 3 * BLK, 0).reshape(
            3, BLK, 2 * HD
        )
        window_ids = global_index + jnp.arange(-1, 2, dtype=jnp.int32)
        window_live = (window_ids >= 0) & (window_ids < total_blocks)
        shared_ids = jnp.concatenate([jnp.clip(window_ids, 0, total_blocks - 1), global_blocks])
        shared_live = jnp.concatenate([window_live, jnp.ones((G,), bool)])
        shared = jnp.concatenate([window, global_kv], axis=0)
        return block_pass(
            query_block,
            grad_block,
            shared,
            shared_live,
            seg_blocks[global_index],
            seg_blocks[shared_ids],
            block_kv,
            seg_blocks[block_ids],
            scaling,
        )

    attended, query_grads, shared_grads, random_grads, log_totals, row_dots = lax.map(
        attend,
        (jnp.arange(qcount, dtype=jnp.int32), query_blocks, grad_blocks, random_kv, random_blocks),
    )
    window_sum = jnp.zeros((qcount + 2, BLK, 2 * HD), jnp.float32)
    for offset in range(3):
        window_sum = window_sum.at[offset : offset + qcount].add(shared_grads[:, offset])
    from_right = from_behind(window_sum[0].astype(jnp.bfloat16), "seq", -1).astype(jnp.float32)
    from_left = from_behind(window_sum[qcount + 1].astype(jnp.bfloat16), "seq", 1).astype(
        jnp.float32
    )
    own_grads = window_sum[1 : qcount + 1]
    own_grads = own_grads.at[qcount - 1].add(from_right).at[0].add(from_left)
    global_sum = lax.psum(jnp.sum(shared_grads[:, 3:], axis=0), "seq")
    global_hits = (
        (global_blocks[:, None] % qcount == jnp.arange(qcount)[None, :]) & owned[:, None]
    ).astype(jnp.float32)
    own_grads = own_grads + jnp.einsum(
        "gq,gkd->qkd", global_hits, global_sum, precision=lax.Precision.HIGHEST
    )
    outgoing = (
        jnp.zeros((devices, capacity, BLK, 2 * HD), jnp.float32)
        .at[owners, slots]
        .set(random_grads.reshape(pick_count, BLK, 2 * HD))
    )
    returned = lax.all_to_all(outgoing, "seq", split_axis=0, concat_axis=0, tiled=True)
    request_hits = (wanted[:, :, None] == jnp.arange(qcount)[None, None, :]).astype(jnp.float32)
    own_grads = own_grads + jnp.einsum(
        "ncq,nckd->qkd", request_hits, returned, precision=lax.Precision.HIGHEST
    )
    own_flat = own_grads.reshape(row_count, 2 * HD)
    return (
        attended.reshape(row_count, HQ * HD),
        query_grads.reshape(row_count, HQ * HD),
        own_flat[:, :HD].astype(jnp.bfloat16),
        own_flat[:, HD:].astype(jnp.bfloat16),
    )


SUM_TYPE = jnp.bfloat16
LOG2E = 1.4426950408889634
DENSE_BYTES = 16 * 1024 * 1024


def attention_kernel(
    random_ref,
    global_ref,
    segment_ref,
    query_ref,
    grad_ref,
    kv_ref,
    kvt_ref,
    attended_ref,
    query_grad_ref,
    sums_ref,
    acc_ref,
):
    wide = jnp.float32
    total_blocks = kv_ref.shape[0]
    qcount = query_ref.shape[0] // BLK
    scaling = 1.0 / math.sqrt(HD)
    first = lax.axis_index("seq") * qcount
    boundary = jnp.sum((segment_ref[...] == segment_ref[0:1, 0:1]).astype(jnp.int32))

    @pl.loop(0, total_blocks)
    def _(index):
        acc_ref[index] = jnp.zeros((BLK, 2 * HD), wide)

    @pl.loop(0, qcount)
    def _(block):
        attend_block(
            block,
            first + block,
            boundary,
            random_ref,
            global_ref,
            query_ref,
            grad_ref,
            kv_ref,
            kvt_ref,
            attended_ref,
            query_grad_ref,
            acc_ref,
        )

    @pl.loop(0, total_blocks)
    def _(index):
        sums_ref[index, :, :HD] = (acc_ref[index, :, :HD] * scaling).astype(sums_ref.dtype)
        sums_ref[index, :, HD:] = acc_ref[index, :, HD:].astype(sums_ref.dtype)


def attend_block(
    block,
    mine,
    boundary,
    random_ref,
    global_ref,
    query_ref,
    grad_ref,
    kv_ref,
    kvt_ref,
    attended_ref,
    query_grad_ref,
    acc_ref,
):
    wide = jnp.float32
    half = jnp.bfloat16
    total_blocks = kv_ref.shape[0]
    heads = HQ
    scaling = 1.0 / math.sqrt(HD)
    rows = pl.ds(pl.multiple_of(block * BLK, BLK), BLK)
    shared_ids = [
        jnp.maximum(mine - 1, 0),
        mine,
        jnp.minimum(mine + 1, total_blocks - 1),
        global_ref[0],
        global_ref[1],
    ]
    dead = [
        jnp.where(mine == 0, masked_value, 0.0).astype(wide),
        None,
        jnp.where(mine == total_blocks - 1, masked_value, 0.0).astype(wide),
        None,
        None,
    ]
    random_ids = [[random_ref[pick, block, head] for head in range(heads)] for pick in range(RAND)]

    queries = [query_ref[rows, head * HD : (head + 1) * HD] for head in range(heads)]
    grads = [grad_ref[rows, head * HD : (head + 1) * HD] for head in range(heads)]
    query_stack = jnp.concatenate(queries, axis=0)
    grad_stack = jnp.concatenate(grads, axis=0)

    def against(rows, columns):
        return lax.dot_general(rows, columns, (((1,), (1,)), ((), ())), preferred_element_type=wide)

    def product(rows, columns):
        return jnp.dot(rows, columns, preferred_element_type=wide)

    def entries(start, stack, parts):
        tiles = [against(kv_ref[i, :, start : start + HD], stack) for i in shared_ids]
        for names in random_ids:
            tiles.append(
                jnp.concatenate(
                    [
                        against(kv_ref[i, :, start : start + HD], part)
                        for i, part in zip(names, parts)
                    ],
                    axis=1,
                )
            )
        return tiles

    key_row = lax.broadcasted_iota(jnp.int32, (BLK, HD), 0)
    query_low = lax.broadcasted_iota(jnp.int32, (BLK, HD), 1) < boundary - mine * BLK

    def allowed(name):
        return (key_row < boundary - name * BLK) == query_low

    scores = entries(0, query_stack, queries)
    factor = scaling * LOG2E
    masked = []
    for slot, tile in enumerate(scores):
        pieces = []
        for head in range(heads):
            piece = tile[:, head * BLK : (head + 1) * BLK] * factor
            name = shared_ids[slot] if slot < 5 else random_ids[slot - 5][head]
            piece = jnp.where(allowed(name), piece, masked_value)
            if slot < 5 and dead[slot] is not None:
                piece = piece + dead[slot]
            pieces.append(piece)
        masked.append(jnp.concatenate(pieces, axis=1))
    top = masked[0]
    for tile in masked[1:]:
        top = jnp.maximum(top, tile)
    top = jnp.max(top, axis=0, keepdims=True)
    powers = [jnp.exp2(tile - top) for tile in masked]
    total = powers[0]
    for tile in powers[1:]:
        total = total + tile
    inverse = 1.0 / jnp.sum(total, axis=0, keepdims=True)
    probs = [tile * inverse for tile in powers]
    probs_half = [tile.astype(half) for tile in probs]

    def gathered(start, tiles):
        shared = product(
            jnp.concatenate([kvt_ref[i, start : start + HD, :] for i in shared_ids], axis=1),
            jnp.concatenate(tiles[:5], axis=0),
        )
        pieces = []
        for head in range(heads):
            names = [random_ids[pick][head] for pick in range(RAND)]
            pieces.append(
                product(
                    jnp.concatenate([kvt_ref[i, start : start + HD, :] for i in names], axis=1),
                    jnp.concatenate(
                        [tile[:, head * BLK : (head + 1) * BLK] for tile in tiles[5:]], axis=0
                    ),
                )
            )
        return shared + jnp.concatenate(pieces, axis=1)

    attended = gathered(HD, probs_half).astype(half).astype(wide)
    grads_turned = jnp.concatenate([part.astype(wide).T for part in grads], axis=1)
    row_dots = jnp.sum(attended * grads_turned, axis=0, keepdims=True)
    for head in range(heads):
        span = slice(head * BLK, (head + 1) * BLK)
        attended_ref[rows, span] = attended[:, span].T.astype(half)
    dprobs = entries(HD, grad_stack, grads)
    dscores = [(p * (d - row_dots)).astype(half) for p, d in zip(probs, dprobs)]
    query_grads = gathered(0, dscores) * scaling
    for head in range(heads):
        span = slice(head * BLK, (head + 1) * BLK)
        query_grad_ref[rows, span] = query_grads[:, span].T.astype(half)
    for slot, name in enumerate(shared_ids):
        acc_ref[name, :, :HD] += product(dscores[slot], query_stack)
        acc_ref[name, :, HD:] += product(probs_half[slot], grad_stack)
    for pick in range(RAND):
        for head in range(heads):
            name = random_ids[pick][head]
            span = slice(head * BLK, (head + 1) * BLK)
            acc_ref[name, :, :HD] += product(dscores[5 + pick][:, span], queries[head])
            acc_ref[name, :, HD:] += product(probs_half[5 + pick][:, span], grads[head])


def attention_call(random_ids, global_ids, segments, queries, out_grads, kv, kvt):
    vmem = pl.BlockSpec(memory_space=pltpu.VMEM)
    smem = pl.BlockSpec(memory_space=pltpu.SMEM)
    return pl.pallas_call(
        attention_kernel,
        in_specs=[smem, smem] + [vmem] * 5,
        out_specs=[vmem] * 3,
        scratch_shapes=[pltpu.VMEM(kv.shape, jnp.float32)],
        out_shape=[
            jax.ShapeDtypeStruct(queries.shape, jnp.bfloat16),
            jax.ShapeDtypeStruct(queries.shape, jnp.bfloat16),
            jax.ShapeDtypeStruct(kv.shape, SUM_TYPE),
        ],
        compiler_params=pltpu.CompilerParams(vmem_limit_bytes=ATTEND_MIB * 1024 * 1024),
        name="block_attention",
    )(random_ids, global_ids, segments, queries, out_grads, kv, kvt)


ATTEND_MIB = 32
LINE = 4
SEQ = 16


class Place:
    def __init__(self):
        me = lax.axis_index("seq")
        self.me = me
        self.core = lax.rem(me, 2)
        self.x = lax.rem(me // 2, 2)
        self.z = me // 4
        self.high = self.z // 2
        self.step = 1 - 2 * self.high
        self.inner = jnp.where((self.z == 1) | (self.z == 2), 1, 0)
        self.partner = self.at(self.z, self.x, 1 - self.core)
        self.across = self.at(self.z, 1 - self.x, self.core)
        self.onward = self.at(self.z + self.step, self.x, self.core)
        self.outward = self.at(self.z - self.step, self.x, self.core)

    def at(self, z, x, core):
        return z * 4 + x * 2 + core


def greet(place):
    barrier = pltpu.get_barrier_semaphore()
    for other in (place.partner, place.across, place.onward):
        pl.semaphore_signal(
            barrier, inc=1, device_id={"seq": other}, device_id_type=pl.DeviceIdType.MESH
        )

    @pl.when(place.inner == 1)
    def _():
        pl.semaphore_signal(
            barrier, inc=1, device_id={"seq": place.outward}, device_id_type=pl.DeviceIdType.MESH
        )

    pl.semaphore_wait(barrier, 3 + place.inner)


def remote(source, target, send, receive, device):
    return pltpu.make_async_remote_copy(
        src_ref=source,
        dst_ref=target,
        send_sem=send,
        recv_sem=receive,
        device_id={"seq": device},
        device_id_type=pl.DeviceIdType.MESH,
    )


def gather_kernel(key_ref, value_ref, out_ref, turned_ref, zs, zr, xs, xr, cs, cr):
    place = Place()
    z, step, inner = place.z, place.step, place.inner
    lines = [z, z + step - 2 * step * inner, z + step * (2 - inner), z + step * (3 - inner)]
    mine = [place.at(line, place.x, place.core) for line in lines]
    theirs = [place.at(line, 1 - place.x, place.core) for line in lines]
    out_ref[place.me, :, :HD] = key_ref[...]
    out_ref[place.me, :, HD:] = value_ref[...]
    greet(place)

    def send(slot, sends, index, receives, to, device):
        return remote(
            out_ref.at[slot], out_ref.at[slot], sends.at[index], receives.at[to], device
        )

    middle = key_ref.shape[0] // 2

    def send_half(slot, start, sends, index, receives, to, device):
        part = out_ref.at[slot, pl.ds(start, middle)]
        return remote(part, part, sends.at[index], receives.at[to], device)

    last = LINE - 1
    detours = [
        send_half(theirs[1], middle, zs, 5, zr, LINE, place.onward),
        send_half(theirs[last], middle, zs, 6, zr, LINE, place.outward),
    ]
    detoured = send_half(theirs[last], middle, zs, 5, zr, LINE, place.onward)
    along = [send(mine[0], zs, 0, zr, 2, place.onward)]
    edge_own = send(mine[0], zs, 0, zr, 1, place.onward)
    out_own = send(mine[0], zs, 1, zr, 1, place.outward)
    relays = [
        send(mine[1], zs, 2, zr, 3, place.onward),
        send(mine[2], zs, 3, zr, 2, place.outward),
        send(mine[3], zs, 4, zr, 3, place.outward),
    ]
    arrivals = [
        send(mine[index], zs, 0, zr, index, place.onward) for index in range(1, LINE)
    ]
    crossing = [send(mine[k], xs, k, xr, k, place.across) for k in range(last)]
    crossing.append(send_half(mine[last], 0, xs, last, xr, last, place.across))
    crossed = [send(theirs[k], xs, k, xr, k, place.across) for k in range(last)]
    crossed.append(send_half(theirs[last], 0, xs, last, xr, last, place.across))
    near = [send(mine[k], cs, k, cr, k, place.partner) for k in range(LINE)]
    far = [send(theirs[k], cs, LINE + k, cr, LINE + k, place.partner) for k in range(LINE)]

    @pl.when(inner == 0)
    def _():
        edge_own.start()

    @pl.when(inner == 1)
    def _():
        along[0].start()
        out_own.start()

    crossing[0].start()
    near[0].start()
    pieces = key_ref.shape[0] // BLK

    def turn(slot):
        for piece in range(pieces):
            rows = slice(piece * BLK, (piece + 1) * BLK)
            turned_ref[slot * pieces + piece] = out_ref[slot, rows, :].T

    def turn_partner(k):
        other = place.at(lines[k], place.x, 1 - place.core)
        other_far = place.at(lines[k], 1 - place.x, 1 - place.core)
        send(other, cs, k, cr, k, place.partner).wait_recv()
        turn(other)
        send(other_far, cs, LINE + k, cr, LINE + k, place.partner).wait_recv()
        turn(other_far)

    for k in range(1, LINE):
        arrivals[k - 1].wait_recv()

        @pl.when(inner == 1)
        def _(k=k):
            relays[k - 1].start()

        crossing[k].start()
        near[k].start()
        turn(mine[k - 1])
        crossed[k - 1].wait_recv()
        far[k - 1].start()
        if k > 1:

            @pl.when(inner == 1)
            def _(k=k):
                if k == last:
                    detoured.wait_recv()
                detours[k - 2].start()

        turn(theirs[k - 1])
        if k > 1:
            turn_partner(k - 2)
    turn(mine[LINE - 1])
    turn_partner(LINE - 2)
    crossed[last].wait_recv()

    @pl.when(inner == 0)
    def _():
        detoured.wait_recv()

    far[last].start()
    turn(theirs[last])
    turn_partner(LINE - 1)
    for k in range(LINE):
        crossing[k].wait_send()
        near[k].wait_send()
        far[k].wait_send()

    edge_own.wait_send()

    @pl.when(inner == 1)
    def _():
        out_own.wait_send()
        for relay in relays + detours:
            relay.wait_send()


def gather_call(keys, values):
    rows = keys.shape[0]
    return pl.pallas_call(
        gather_kernel,
        in_specs=[pl.BlockSpec(memory_space=pltpu.VMEM)] * 2,
        out_specs=[pl.BlockSpec(memory_space=pltpu.VMEM)] * 2,
        out_shape=[
            jax.ShapeDtypeStruct((SEQ, rows, 2 * HD), keys.dtype),
            jax.ShapeDtypeStruct((SEQ * rows // BLK, 2 * HD, BLK), keys.dtype),
        ],
        scratch_shapes=[
            pltpu.SemaphoreType.DMA((7,)),
            pltpu.SemaphoreType.DMA((LINE + 1,)),
            pltpu.SemaphoreType.DMA((LINE,)),
            pltpu.SemaphoreType.DMA((LINE,)),
            pltpu.SemaphoreType.DMA((2 * LINE,)),
            pltpu.SemaphoreType.DMA((2 * LINE,)),
        ],
        compiler_params=pltpu.CompilerParams(
            collective_id=0, has_side_effects=True, vmem_limit_bytes=32 * 1024 * 1024
        ),
        name="gather_blocks",
    )(keys, values)


def scatter_kernel(
    sums_ref, key_ref, value_ref, pair, cross_out, cross_in, line_out, line_in,
    ps, pr, xs, xr, zs, zr,
):
    place = Place()
    z, high, inner = place.z, place.high, place.inner
    wide = jnp.float32
    order = [3 * (1 - high), 2 - high, 1 - z + 4 * high, z]
    greet(place)

    def paired(side, k):
        x = 1 - place.x if side == 0 else place.x
        index = side * LINE + k
        source = sums_ref.at[place.at(order[k], x, 1 - place.core)]
        return remote(source, pair.at[index], ps.at[index], pr.at[index], place.partner)

    pairs = [[paired(side, k) for k in range(LINE)] for side in range(2)]
    crosses = [
        remote(cross_out.at[k], cross_in.at[k], xs.at[k], xr.at[k], place.across)
        for k in range(LINE)
    ]

    def hop(k, slot, device):
        return remote(line_out.at[k], line_in.at[slot], zs.at[k], zr.at[slot], device)

    for side in range(2):
        for k in range(LINE):
            pairs[side][k].start()
    for k in range(LINE):
        pairs[0][k].wait_recv()
        kept = sums_ref[place.at(order[k], 1 - place.x, place.core)]
        cross_out[k] = (kept.astype(wide) + pair[k].astype(wide)).astype(cross_out.dtype)
        crosses[k].start()

    def local(k):
        kept = sums_ref[place.at(order[k], place.x, place.core)].astype(wide)
        return kept + pair[LINE + k].astype(wide) + cross_in[k].astype(wide)

    def arrived(slot):
        hop(0, slot, place.onward).wait_recv()
        return line_in[slot].astype(wide)

    for k in range(LINE - 1):
        pairs[1][k].wait_recv()
        crosses[k].wait_recv()

        @pl.when(inner == 0)
        def _(k=k):
            line_out[k] = local(k).astype(line_out.dtype)
            hop(k, k, place.onward).start()

        @pl.when(inner == 1)
        def _(k=k):
            total = local(k) + arrived(k if k < 2 else 3)
            line_out[k] = total.astype(line_out.dtype)
            if k < 2:
                hop(k, 3 + k, place.onward).start()
            else:
                hop(k, 0, place.outward).start()

    pairs[1][LINE - 1].wait_recv()
    crosses[LINE - 1].wait_recv()

    def finish(total):
        key_ref[...] = total[:, :HD].astype(key_ref.dtype)
        value_ref[...] = total[:, HD:].astype(value_ref.dtype)

    @pl.when(inner == 0)
    def _():
        finish(local(LINE - 1) + arrived(0))

    @pl.when(inner == 1)
    def _():
        finish(local(LINE - 1) + arrived(2) + arrived(4))

    for k in range(LINE):
        pairs[0][k].wait_send()
        pairs[1][k].wait_send()
        crosses[k].wait_send()
    for k in range(LINE - 1):
        hop(k, k, place.onward).wait_send()


def scatter_call(sums):
    rows = sums.shape[1]
    half = jnp.bfloat16

    def slots(count):
        return pltpu.VMEM((count, rows, 2 * HD), half)

    return pl.pallas_call(
        scatter_kernel,
        in_specs=[pl.BlockSpec(memory_space=pltpu.VMEM)],
        out_specs=[pl.BlockSpec(memory_space=pltpu.VMEM)] * 2,
        out_shape=[jax.ShapeDtypeStruct((rows, HD), half)] * 2,
        scratch_shapes=[
            slots(2 * LINE),
            slots(LINE),
            slots(LINE),
            slots(LINE - 1),
            slots(5),
            pltpu.SemaphoreType.DMA((2 * LINE,)),
            pltpu.SemaphoreType.DMA((2 * LINE,)),
            pltpu.SemaphoreType.DMA((LINE,)),
            pltpu.SemaphoreType.DMA((LINE,)),
            pltpu.SemaphoreType.DMA((LINE - 1,)),
            pltpu.SemaphoreType.DMA((5,)),
        ],
        compiler_params=pltpu.CompilerParams(
            collective_id=1, has_side_effects=True, vmem_limit_bytes=40 * 1024 * 1024
        ),
        name="scatter_sums",
    )(sums)


def dense_body(queries, key_rows, value_rows, out_grads, segment_ids, random_blocks, global_blocks):
    total_blocks = segment_ids.shape[0] // BLK
    kv, kvt = gather_call(key_rows, value_rows)
    kv = kv.reshape(total_blocks, BLK, 2 * HD)
    attended, query_grads, sums = attention_call(
        random_blocks.transpose(2, 0, 1), global_blocks, segment_ids.reshape(total_blocks, BLK), queries,
        out_grads, kv, kvt,
    )
    key_grads, value_grads = scatter_call(sums.reshape(SEQ, -1, 2 * HD))
    return (attended, query_grads, key_grads, value_grads)


def plan(*arrays):
    tokens = arrays[4].shape[0]
    fits = tokens * 2 * HD * 4 <= DENSE_BYTES
    chosen = dense_body if fits and lax.axis_size("seq") == SEQ else body
    return chosen(*arrays)


def solution(mesh):
    placed = (
        P(("shard", "seq"), None),
        P(("shard", "seq"), None),
        P(("shard", "seq"), None),
        P(("shard", "seq"), None),
        P("shard"),
        P(("shard", "seq"), None, None),
        P("shard"),
    )
    return jax.shard_map(
        plan,
        mesh=mesh,
        in_specs=placed,
        out_specs=(
            P(("shard", "seq"), None),
            P(("shard", "seq"), None),
            P(("shard", "seq"), None),
            P(("shard", "seq"), None),
        ),
        check_vma=False,
    )
```
